256 devices in a mesh: dp: 64 (over z, x, core), tensor: 4 (over y).
Axes of the slice: x: 4, y: 4, z: 8, core: 2. Of those that a mesh axis runs over, the one named last changes fastest.
Arguments:
- tokens: bfloat16 [32768, 8192], P('dp', 'tensor'), may hold values from -6 to 6
- cotangent: bfloat16 [32768, 1024], P('dp', 'tensor'), may hold values from -6 to 6
- frozen_key_weight: bfloat16 [8192, 1024], P(None, 'tensor'), may hold values from -0.0625 to 0.0625
- counts: int32 [64, 64], P('dp'), may hold values from 1 to 12, 512 in all within a row
- holder_assignment: int32 [64], replicated, may hold values from 0 to 63, each once
- adapter_down_matrix: float32 [64, 64, 8192], P('dp', None, 'tensor'), may hold values from -0.0625 to 0.0625
- adapter_up_matrix: float32 [64, 64, 1024], P('dp', None, 'tensor'), may hold values from -0.06 to 0.06
- down_first_moment: float32 [64, 64, 8192], P('dp', None, 'tensor'), may hold values from -12 to 12
- down_second_moment: float32 [64, 64, 8192], P('dp', None, 'tensor'), may hold values from 1 to 100
- up_first_moment: float32 [64, 64, 1024], P('dp', None, 'tensor'), may hold values from -30 to 30
- up_second_moment: float32 [64, 64, 1024], P('dp', None, 'tensor'), may hold values from 10 to 1000
Outputs:
- layer_out: bfloat16 [32768, 1024], P('dp', 'tensor')
- input_grad: bfloat16 [32768, 8192], P('dp', 'tensor')
- fresh_down_matrix: float32 [64, 64, 8192], P('dp', None, 'tensor')
- fresh_down_first: float32 [64, 64, 8192], P('dp', None, 'tensor')
- fresh_down_second: float32 [64, 64, 8192], P('dp', None, 'tensor')
- fresh_up_matrix: float32 [64, 64, 1024], P('dp', None, 'tensor')
- fresh_up_first: float32 [64, 64, 1024], P('dp', None, 'tensor')
- fresh_up_second: float32 [64, 64, 1024], P('dp', None, 'tensor')
The draws below stay inside these ranges and needn't reach their ends.
Inputs may be any that keep to these rules, and one draw needn't show every extreme that they name: `counts`: row j gives, adapter by adapter in order, how many of dp index j's tokens belong to each adapter; dp index j's rows of tokens and cotangent are grouped in that order; each row sums to 512, and some entry of each row equals 12. A permutation: holder_assignment[a] is the dp index that holds adapter a.
All inputs are finite; a program needn't handle non-finite values.
Results may differ from the reference program's by a relative error of at most 0.0021.
Values may be sent and summed in bfloat16 or wider, within the bound.
No kernel may reach another device: no remote copies, remote signals or barrier semaphores. Data moves between devices by JAX's collectives and lax.ppermute only.
A program may use at most 128 MiB of HBM per device.

```python
import math
import jax
import jax.numpy as jnp
import numpy as np
from jax import lax

MODEL_WIDTH = 8192
KEY_OUTPUTS = 1024
ADAPTER_RANK = 64
TOK_DEV = 512
ADAPTER_COUNT = 64
CAP = 12
TOKENS = 32768
N_DP = 64


def shard_levels(rng, dims, shards, least, largest):
    def one(position, blocks):
        draws = jax.random.uniform(jax.random.fold_in(jax.random.fold_in(rng, 6), position), (blocks,), jnp.float32, least / len(shards), largest / len(shards))
        return jnp.repeat(jnp.exp(draws), dims[position] // blocks).reshape((-1,) + (1,) * (len(dims) - position - 1))

    gain = one(*shards[0])
    for cut in shards[1:]:
        gain = gain * one(*cut)
    return gain


def length_profile(count, total, most, lean):
    weights = [(1 << 20) // math.isqrt(grade ** lean) + 1 for grade in range(2, count + 1)]
    spare, given = total - most - (count - 1), [1] * (count - 1)
    while spare > 0:
        movable = [i for i in range(count - 1) if given[i] < most]
        whole, budget = sum([weights[i] for i in movable]), spare
        for i in movable:
            addition = min(most - given[i], max(1, budget * weights[i] // whole), spare)
            given[i] = given[i] + addition
            spare = spare - addition
    return np.array([most] + given)


def uneven(stream_key, amount, total, reach, skew):
    if amount == 2:
        one = jax.random.randint(stream_key, (), max(1, total - reach), min(reach, total - 1) + 1)
        return jnp.stack([one, total - one])
    tallies = jnp.asarray(length_profile(amount, total, reach, skew), jnp.int32)
    twos = (amount - 1) // 2
    donor, receiver = tallies[1:1 + 2 * twos:2], tallies[2:2 + 2 * twos:2]
    margin = jnp.minimum(donor - 1, reach - receiver)
    passed = jax.random.randint(jax.random.fold_in(stream_key, 1), (twos,), 0, 1 << 20) % (margin + 1)
    tallies = tallies.at[1:1 + 2 * twos:2].set(donor - passed).at[2:2 + 2 * twos:2].set(receiver + passed)
    return tallies[jax.random.permutation(jax.random.fold_in(stream_key, 2), amount)]


def scatter_about(key, shape, scale, bound, shards=(), held_as=jnp.bfloat16):
    drawn = scale * jax.random.normal(key, shape, jnp.float32)
    if shards:
        drawn = drawn * shard_levels(key, shape, shards, -0.22, 0.18)
    return jnp.clip(drawn, -bound, bound).astype(held_as)


def setup_inputs(seed: int = 0) -> dict:
    keys = jax.random.split(jax.random.key(seed), 12)
    tokens = scatter_about(keys[0], (TOKENS, MODEL_WIDTH), 1.0, 6.0, ((0, 64), (1, 4)))
    cotangent = scatter_about(keys[1], (TOKENS, KEY_OUTPUTS), 1.0, 6.0, ((0, 64), (1, 4)))
    frozen_key_weight = scatter_about(keys[2], (MODEL_WIDTH, KEY_OUTPUTS), MODEL_WIDTH ** -0.5, 0.0625, ((1, 4),))
    counts = jax.vmap(lambda own: uneven(own, ADAPTER_COUNT, TOK_DEV, CAP, 2))(jax.random.split(keys[3], N_DP)).reshape((N_DP, ADAPTER_COUNT)).astype(jnp.int32)
    holder_assignment = jax.random.permutation(keys[4], ADAPTER_COUNT).astype(jnp.int32)
    adapter_down_matrix = scatter_about(keys[5], (ADAPTER_COUNT, ADAPTER_RANK, MODEL_WIDTH), MODEL_WIDTH ** -0.5, 0.0625, ((0, 64), (2, 4)), jnp.float32)
    adapter_up_matrix = scatter_about(keys[6], (ADAPTER_COUNT, ADAPTER_RANK, KEY_OUTPUTS), 0.01, 0.06, ((0, 64), (2, 4)), jnp.float32)
    down_first_moment = scatter_about(keys[7], (ADAPTER_COUNT, ADAPTER_RANK, MODEL_WIDTH), 2.0, 12.0, ((0, 64), (2, 4)), jnp.float32)
    down_second_moment = jnp.clip(jnp.exp(math.log(100.0) - 4.6051702 * jax.random.uniform(keys[8], (ADAPTER_COUNT, ADAPTER_RANK, MODEL_WIDTH), jnp.float32) ** shard_levels(keys[8], (ADAPTER_COUNT, ADAPTER_RANK, MODEL_WIDTH), ((0, 64), (2, 4)), -0.2, 0.2)), 1.0, 100.0)
    up_first_moment = scatter_about(keys[9], (ADAPTER_COUNT, ADAPTER_RANK, KEY_OUTPUTS), 5.0, 30.0, ((0, 64), (2, 4)), jnp.float32)
    up_second_moment = jnp.clip(jnp.exp(math.log(1000.0) - 4.6051702 * jax.random.uniform(keys[10], (ADAPTER_COUNT, ADAPTER_RANK, KEY_OUTPUTS), jnp.float32) ** shard_levels(keys[10], (ADAPTER_COUNT, ADAPTER_RANK, KEY_OUTPUTS), ((0, 64), (2, 4)), -0.2, 0.2)), 10.0, 1000.0)
    return {"tokens": tokens, "cotangent": cotangent, "frozen_key_weight": frozen_key_weight, "counts": counts, "holder_assignment": holder_assignment, "adapter_down_matrix": adapter_down_matrix, "adapter_up_matrix": adapter_up_matrix, "down_first_moment": down_first_moment, "down_second_moment": down_second_moment, "up_first_moment": up_first_moment, "up_second_moment": up_second_moment}


adapter_scale = 2.0
learn_rate = 0.01
beta_one = 0.9
beta_two = 0.999
adam_eps = 1e-08
adam_step = 10

def optimizer_update(weight, moment, second, grad):
    moment_new = beta_one * moment + (1.0 - beta_one) * grad
    second_new = beta_two * second + (1.0 - beta_two) * grad * grad
    first_fix = 1.0 - beta_one ** adam_step
    second_fix = 1.0 - beta_two ** adam_step
    weight_new = weight - learn_rate * (moment_new / first_fix) / (jnp.sqrt(second_new / second_fix) + adam_eps)
    return (weight_new, moment_new, second_new)

def reference(tokens, cotangent, frozen_key_weight, counts, holder_assignment, adapter_down_matrix, adapter_up_matrix, down_first_moment, down_second_moment, up_first_moment, up_second_moment):
    base_out = jnp.dot(tokens, frozen_key_weight, preferred_element_type=jnp.float32)
    base_grad = jnp.dot(cotangent, frozen_key_weight.T, preferred_element_type=jnp.float32)
    upper = jnp.cumsum(counts, axis=1).astype(jnp.int32)
    lower = (upper - counts).astype(jnp.int32)
    adapter_iota = jnp.arange(ADAPTER_COUNT, dtype=jnp.int32)
    inverse = lax.optimization_barrier(jnp.sum(jnp.where(holder_assignment[None, :] == adapter_iota[:, None], adapter_iota[None, :], 0), axis=1)).astype(jnp.int32)
    slot_iota = jnp.arange(CAP, dtype=jnp.int32)
    source_iota = jnp.arange(N_DP, dtype=jnp.int32)

    def owner_step(carry, holder_index):
        extra_out, extra_grad = carry
        adapter = inverse[holder_index]
        start_rows = lower[:, adapter]
        live_count = counts[:, adapter]
        live = slot_iota[None, :] < live_count[:, None]
        index = jnp.where(live, source_iota[:, None] * TOK_DEV + start_rows[:, None] + slot_iota[None, :], 0)
        index = index.reshape(-1).astype(jnp.int32)
        keep = live.reshape(-1)[:, None]
        x_rows = jnp.where(keep, tokens[index], jnp.zeros((), tokens.dtype))
        gradient_rows = jnp.where(keep, cotangent[index], jnp.zeros((), cotangent.dtype))
        down_half16 = adapter_down_matrix[holder_index].astype(jnp.bfloat16)
        up_half16 = adapter_up_matrix[holder_index].astype(jnp.bfloat16)
        hidden = jnp.dot(x_rows, down_half16.T, preferred_element_type=jnp.float32)
        hidden_backward = adapter_scale * jnp.dot(gradient_rows, up_half16.T, preferred_element_type=jnp.float32)
        hidden_half16 = hidden.astype(jnp.bfloat16)
        back16 = hidden_backward.astype(jnp.bfloat16)
        adapter_output = (adapter_scale * jnp.dot(hidden_half16, up_half16, preferred_element_type=jnp.float32)).astype(jnp.bfloat16)
        adapter_grad = jnp.dot(back16, down_half16, preferred_element_type=jnp.float32).astype(jnp.bfloat16)
        down_gradient = jnp.dot(back16.T, x_rows, preferred_element_type=jnp.float32)
        up_gradient = adapter_scale * jnp.dot(hidden_half16.T, gradient_rows, preferred_element_type=jnp.float32)
        extra_out = extra_out.at[index].add(jnp.where(keep, adapter_output, jnp.zeros((), adapter_output.dtype)))
        extra_grad = extra_grad.at[index].add(jnp.where(keep, adapter_grad, jnp.zeros((), adapter_grad.dtype)))
        return ((extra_out, extra_grad), (down_gradient, up_gradient))
    start_carry = (jnp.zeros((TOKENS, KEY_OUTPUTS), jnp.bfloat16), jnp.zeros((TOKENS, MODEL_WIDTH), jnp.bfloat16))
    (extra_out, extra_grad), (down_gradient, up_gradient) = lax.scan(owner_step, start_carry, adapter_iota)
    layer_out = (base_out + extra_out.astype(jnp.float32)).astype(jnp.bfloat16)
    input_grad = (base_grad + extra_grad.astype(jnp.float32)).astype(jnp.bfloat16)
    fresh_down_matrix, fresh_down_first, fresh_down_second = optimizer_update(adapter_down_matrix, down_first_moment, down_second_moment, down_gradient)
    fresh_up_matrix, fresh_up_first, fresh_up_second = optimizer_update(adapter_up_matrix, up_first_moment, up_second_moment, up_gradient)
    return (layer_out, input_grad, fresh_down_matrix, fresh_down_first, fresh_down_second, fresh_up_matrix, fresh_up_first, fresh_up_second)
```

```python
import jax
import jax.numpy as jnp
from jax import lax
from jax.sharding import Mesh, PartitionSpec as P


adapter_scale = 2.0
learn_rate = 0.01
beta_one = 0.9
beta_two = 0.999
adam_eps = 1e-08
adam_step = 10

NZ, NX, NC, NT = 8, 4, 2, 4
NS = NX * NC
CAP = 12
ROWS = NZ * CAP


bf16 = jnp.bfloat16
f32 = jnp.float32


def optimizer_update(weight, moment, second, grad):
    moment_new = beta_one * moment + (1.0 - beta_one) * grad
    second_new = beta_two * second + (1.0 - beta_two) * grad * grad
    first_fix = 1.0 - beta_one**adam_step
    second_fix = 1.0 - beta_two**adam_step
    weight_new = weight - learn_rate * (moment_new / first_fix) / (
        jnp.sqrt(second_new / second_fix) + adam_eps
    )
    return (weight_new, moment_new, second_new)


def shift(v, k):
    return lax.ppermute(v, "t", [(i, (i + k) % NT) for i in range(NT)])


def exchange(v, axes, n, me):
    size = v.shape[0] // n
    got = []
    for k in range(n):
        block = lax.dynamic_slice(v, (((me + k) % n) * size, 0), (size, v.shape[1]))
        got.append(lax.ppermute(block, axes, [(i, (i + k) % n) for i in range(n)]) if k else block)
    back = [got[-j % n] for j in range(n)]
    return lax.dynamic_slice(
        jnp.concatenate(back + back[: n - 1], axis=0), (((n - me) % n) * size, 0), v.shape
    )


def dot(a, b, dims=((1,), (0,)), out=f32):
    return lax.dot_general(a, b, (dims, ((), ())), preferred_element_type=out)


def step(
    tokens,
    cotangent,
    frozen_key_weight,
    counts,
    holder_assignment,
    adapter_down_matrix,
    adapter_up_matrix,
    down_first_moment,
    down_second_moment,
    up_first_moment,
    up_second_moment,
):
    tok_rows, feat = tokens.shape
    keyw = cotangent.shape[1]
    rank = adapter_down_matrix.shape[1]
    t = lax.axis_index("t")
    c = lax.axis_index("c")
    xc = lax.axis_index(("x", "c"))
    z = lax.axis_index("z")

    both16 = jnp.concatenate([adapter_down_matrix[0], adapter_up_matrix[0]], axis=1).astype(bf16)
    all16 = lax.all_gather(both16, "z", axis=0, tiled=True)
    down_all = all16[:, :feat]
    up_all = all16[:, feat:]

    own_counts = counts[0]
    upper = jnp.cumsum(own_counts)
    lower = upper - own_counts
    slot = jnp.arange(NS * ROWS, dtype=jnp.int32)
    slot_owner = (slot % ROWS) // CAP * NS + slot // ROWS
    slot_k = slot % CAP
    pick = holder_assignment[None, :] == slot_owner[:, None]
    start = jnp.sum(jnp.where(pick, lower[None, :], 0), axis=1)
    count = jnp.sum(jnp.where(pick, own_counts[None, :], 0), axis=1)
    source = jnp.where(slot_k < count, start + slot_k, -1)
    route = (source[:, None] == jnp.arange(tok_rows, dtype=jnp.int32)[None, :]).astype(bf16)

    x_send = dot(route, tokens, out=bf16)
    x_rows = lax.all_to_all(x_send, ("x", "c"), 0, 0, tiled=True)
    g_send = dot(route, cotangent, out=bf16)
    g_rows = exchange(g_send, ("x", "c"), NS, xc)

    half = feat // NC
    halves = []
    for k in range(1, NT):
        piece = lax.dynamic_slice(
            frozen_key_weight, (((t + k) % NT) * feat + c * half, 0), (half, keyw)
        )
        halves.append(shift(piece, k))
    mine = jnp.concatenate(halves, axis=0)
    other = lax.ppermute(mine, "c", [(0, 1), (1, 0)])
    first = jnp.where(c == 0, mine, other).reshape(NT - 1, half, keyw)
    last = jnp.where(c == 0, other, mine).reshape(NT - 1, half, keyw)
    own_w = lax.dynamic_slice(frozen_key_weight, (t * feat, 0), (feat, keyw))
    weights = [own_w] + [jnp.concatenate([first[k], last[k]], axis=0) for k in range(NT - 1)]
    cots = [cotangent] + [shift(cotangent, k) for k in range(1, NT)]
    base_grad = dot(
        jnp.concatenate(cots, axis=1), jnp.concatenate(weights, axis=1), ((1,), (1,))
    )
    base_out = dot(tokens, own_w)
    for k in range(1, NT):
        base_out = base_out + shift(dot(tokens, weights[k]), -k)

    row = lax.broadcasted_iota(jnp.int32, (NS * ROWS, NZ * rank), 0)
    col = lax.broadcasted_iota(jnp.int32, (NS * ROWS, NZ * rank), 1)
    block = (row % ROWS) // CAP == col // rank
    pair = 2 * rank
    mid = NS * ROWS // 2

    def reduced(v):
        own = jnp.sum(jnp.where(block, v, 0.0).reshape(NS * ROWS, -1, pair), axis=1)
        own = own[:mid] + jnp.roll(own[mid:], rank, axis=1)
        total = own
        for k in range(1, NT):
            total = total + shift(own, k)
        return total

    def spread(total):
        total = total.astype(bf16)
        both = jnp.concatenate([total, jnp.roll(total, rank, axis=1)], axis=0)
        return jnp.where(block, jnp.tile(both, (1, NZ // 2)), jnp.zeros((), bf16))

    back16 = spread(adapter_scale * reduced(dot(g_rows, up_all, ((1,), (1,)))))
    adapter_grad = dot(back16, down_all, out=bf16)
    ret_grad = lax.all_to_all(adapter_grad, ("x", "c"), 0, 0, tiled=True)
    grad_down = lax.psum_scatter(
        dot(back16, x_rows, ((0,), (0,))), "z", scatter_dimension=0, tiled=True
    )

    hidden16 = spread(reduced(dot(x_rows, down_all, ((1,), (1,)))))
    adapter_out = (adapter_scale * dot(hidden16, up_all)).astype(bf16)
    ret_out = exchange(adapter_out, ("x", "c"), NS, xc)
    up_part = dot(hidden16, g_rows, ((0,), (0,)))
    grad_up = lax.dynamic_slice(up_part, (z * rank, 0), (rank, keyw))
    for k in range(1, NZ):
        block_k = lax.dynamic_slice(up_part, (((z + k) % NZ) * rank, 0), (rank, keyw))
        grad_up = grad_up + lax.ppermute(
            block_k, "z", [(i, (i + k) % NZ) for i in range(NZ)]
        )

    layer_out = (base_out + dot(route, ret_out, ((0,), (0,)))).astype(bf16)
    input_grad = (base_grad + dot(route, ret_grad, ((0,), (0,)))).astype(bf16)
    fresh_down = optimizer_update(
        adapter_down_matrix[0], down_first_moment[0], down_second_moment[0], grad_down
    )
    fresh_up = optimizer_update(
        adapter_up_matrix[0], up_first_moment[0], up_second_moment[0], adapter_scale * grad_up
    )
    return (layer_out, input_grad) + tuple(v[None] for v in fresh_down + fresh_up)


def solution(mesh):
    split = Mesh(mesh.devices.reshape(NZ, NX, NC, NT), ("z", "x", "c", "t"))
    dp = ("z", "x", "c")
    act = P(dp, "t")
    state = P(dp, None, "t")
    return jax.shard_map(
        step,
        mesh=split,
        in_specs=(act, act, P(None, "t"), P(dp, None), P()) + (state,) * 6,
        out_specs=(act, act) + (state,) * 6,
        check_vma=False,
    )
```

```python
import jax
import jax.numpy as jnp
from jax import lax
from jax.experimental import pallas as pl
from jax.experimental.pallas import tpu as pltpu
from jax.sharding import Mesh, PartitionSpec as P


adapter_scale = 2.0
learn_rate = 0.01
beta_one = 0.9
beta_two = 0.999
adam_eps = 1e-08
adam_step = 10

NZ, NX, NC, NT = 8, 4, 2, 4
NS = NX * NC
CAP = 12
ROWS = NZ * CAP


bf16 = jnp.bfloat16
f32 = jnp.float32
R = NS * ROWS
MID = R // 2
RANK = 64
PAIR = 2 * RANK
WIDE = NZ * RANK


def optimizer_update(weight, moment, second, grad):
    moment_new = beta_one * moment + (1.0 - beta_one) * grad
    second_new = beta_two * second + (1.0 - beta_two) * grad * grad
    first_fix = 1.0 - beta_one**adam_step
    second_fix = 1.0 - beta_two**adam_step
    weight_new = weight - learn_rate * (moment_new / first_fix) / (
        jnp.sqrt(second_new / second_fix) + adam_eps
    )
    return (weight_new, moment_new, second_new)


def shift(v, k):
    return lax.ppermute(v, "t", [(i, (i + k) % NT) for i in range(NT)])


def dot(a, b, dims=((1,), (0,)), out=f32):
    return lax.dot_general(a, b, (dims, ((), ())), preferred_element_type=out)


def call(body, outs, specs=None, out_specs=None, grid=(), scratch=()):
    vm = pl.BlockSpec(memory_space=pltpu.VMEM)
    kw = {}
    if grid:
        kw["grid"] = grid
    one = not isinstance(outs, (tuple, list))
    return pl.pallas_call(
        body,
        out_shape=outs,
        in_specs=specs,
        out_specs=out_specs or (vm if one else [vm] * len(outs)),
        scratch_shapes=list(scratch),
        **kw,
    )


VM = pl.BlockSpec(memory_space=pltpu.VMEM)


def whole(shape):
    return pl.BlockSpec(shape, lambda *_: (0,) * len(shape))


def row_mask():
    r = lax.broadcasted_iota(jnp.int32, (ROWS, WIDE), 0)
    first = lax.shift_right_logical(lax.broadcasted_iota(jnp.int32, (ROWS, WIDE), 1), 6) * CAP
    return (r >= first) & (r < first + CAP)


def fold(v):
    mask = row_mask()
    rows = []
    for s in range(NS):
        m = jnp.where(mask, v[s * ROWS : (s + 1) * ROWS], 0.0)
        rows.append(sum(m[:, q * PAIR : (q + 1) * PAIR] for q in range(1, NZ // 2)) + m[:, :PAIR])
    half = NS // 2
    return jnp.concatenate(
        [rows[s] + pltpu.roll(rows[s + half], RANK, 1) for s in range(half)], axis=0
    )


def spread_rows(total, out_ref):
    mask = row_mask()
    both = (total, pltpu.roll(total, RANK, 1))
    for s in range(NS):
        half, at = s // (NS // 2), s % (NS // 2) * ROWS
        v = both[half][at : at + ROWS]
        out_ref[pl.ds(s * ROWS, ROWS), :] = jnp.where(
            mask, jnp.concatenate([v] * (NZ // 2), axis=1), 0.0
        ).astype(bf16)


def spread_cols(total, out_ref):
    lo = total.T
    hi = jnp.concatenate([lo[RANK:], lo[:RANK]], axis=0)
    both = jnp.concatenate([lo, hi], axis=1)
    col = lax.broadcasted_iota(jnp.int32, (RANK, R), 1)
    for s in range(1, NS):
        col = jnp.where(lax.broadcasted_iota(jnp.int32, (RANK, R), 1) >= s * ROWS, col - ROWS, col)
    for a in range(NZ):
        keep = (col >= a * CAP) & (col < (a + 1) * CAP)
        v = both[(a % 2) * RANK : (a % 2 + 1) * RANK]
        out_ref[pl.ds(a * RANK, RANK), :] = jnp.where(keep, v, 0.0).astype(bf16)


def back_kernel(g, up, out):
    out[...] = fold(dot(g[...], up[...], ((1,), (1,))))


def grad_kernel(a, b, c, d, x, back16, grad, cols):
    @pl.when(pl.program_id(0) == 0)
    def _():
        total = adapter_scale * (a[...] + b[...] + c[...] + d[...])
        spread_rows(total, back16)
        spread_cols(total, cols)

    grad[...] = dot(cols[...], x[...])


def adg_kernel(back16, down, out):
    out[...] = dot(back16[...], down[...]).astype(bf16)


def hid_kernel(x, down, out, acc):
    @pl.when(pl.program_id(0) == 0)
    def _():
        acc[...] = jnp.zeros_like(acc)

    acc[...] += dot(x[...], down[...], ((1,), (1,)))

    @pl.when(pl.program_id(0) == pl.num_programs(0) - 1)
    def _():
        out[...] = fold(acc[...])


def up_kernel(a, b, c, d, g, up, out, grad, rows, cols):
    total = a[...] + b[...] + c[...] + d[...]
    spread_rows(total, rows)
    spread_cols(total, cols)
    out[...] = (adapter_scale * dot(rows[...], up[...])).astype(bf16)
    grad[...] = dot(cols[...], g[...])


def base_kernel(c, tokens, own, m1, m2, m3, o1, o2, o3, w, p0, p1, p2, p3):
    half = m1.shape[0]
    keyw = m1.shape[1]
    w[:, :keyw] = own[...]
    for k, (m, o) in enumerate(((m1, o1), (m2, o2), (m3, o3))):
        cols = pl.ds((k + 1) * keyw, keyw)

        @pl.when(c[0] == 0)
        def _():
            w[:half, cols] = m[...]
            w[half:, cols] = o[...]

        @pl.when(c[0] == 1)
        def _():
            w[:half, cols] = o[...]
            w[half:, cols] = m[...]

    for k, p in enumerate((p0, p1, p2, p3)):
        p[...] = dot(tokens[...], w[:, k * keyw : (k + 1) * keyw])


def run_back(g_rows, all16, feat, keyw):
    return call(
        back_kernel,
        jax.ShapeDtypeStruct((MID, PAIR), f32),
        [whole((R, keyw)), pl.BlockSpec((WIDE, keyw), lambda i: (0, feat // keyw))],
        whole((MID, PAIR)),
        (1,),
    )(g_rows, all16)


def run_grad(parts, x_rows):
    feat = x_rows.shape[1]
    nb = 4
    return call(
        grad_kernel,
        [jax.ShapeDtypeStruct((R, WIDE), bf16), jax.ShapeDtypeStruct((WIDE, feat), f32)],
        [whole((MID, PAIR))] * 4 + [pl.BlockSpec((R, feat // nb), lambda j: (0, j))],
        [whole((R, WIDE)), pl.BlockSpec((WIDE, feat // nb), lambda j: (0, j))],
        (nb,),
        [pltpu.VMEM((WIDE, R), bf16)],
    )(*parts, x_rows)


def run_adg(back16, all16, feat):
    nb = 4
    return call(
        adg_kernel,
        jax.ShapeDtypeStruct((R, feat), bf16),
        [whole((R, WIDE)), pl.BlockSpec((WIDE, feat // nb), lambda j: (0, j))],
        pl.BlockSpec((R, feat // nb), lambda j: (0, j)),
        (nb,),
    )(back16, all16)


def run_hid(x_rows, all16):
    feat = x_rows.shape[1]
    nb = 4
    return call(
        hid_kernel,
        jax.ShapeDtypeStruct((MID, PAIR), f32),
        [
            pl.BlockSpec((R, feat // nb), lambda j: (0, j)),
            pl.BlockSpec((WIDE, feat // nb), lambda j: (0, j)),
        ],
        whole((MID, PAIR)),
        (nb,),
        [pltpu.VMEM((R, WIDE), f32)],
    )(x_rows, all16)


def run_up(parts, g_rows, all16, feat):
    keyw = g_rows.shape[1]
    return call(
        up_kernel,
        [jax.ShapeDtypeStruct((R, keyw), bf16), jax.ShapeDtypeStruct((WIDE, keyw), f32)],
        [whole((MID, PAIR))] * 4
        + [whole((R, keyw)), pl.BlockSpec((WIDE, keyw), lambda i: (0, feat // keyw))],
        [whole((R, keyw)), whole((WIDE, keyw))],
        (1,),
        [pltpu.VMEM((R, WIDE), bf16), pltpu.VMEM((WIDE, R), bf16)],
    )(*parts, g_rows, all16)


def run_base(c, tokens, own, mine, other):
    rows, feat = tokens.shape
    keyw = own.shape[1]
    return call(
        base_kernel,
        [jax.ShapeDtypeStruct((feat, NT * keyw), bf16)]
        + [jax.ShapeDtypeStruct((rows, keyw), f32)] * NT,
        [pl.BlockSpec(memory_space=pltpu.SMEM)] + [VM] * 8,
        [VM] * (1 + NT),
    )(c.reshape(1), tokens, own, *mine, *other)


def step(
    tokens,
    cotangent,
    frozen_key_weight,
    counts,
    holder_assignment,
    adapter_down_matrix,
    adapter_up_matrix,
    down_first_moment,
    down_second_moment,
    up_first_moment,
    up_second_moment,
):
    tok_rows, feat = tokens.shape
    keyw = cotangent.shape[1]
    rank = adapter_down_matrix.shape[1]
    t = lax.axis_index("t")
    c = lax.axis_index("c")

    both16 = jnp.concatenate([adapter_down_matrix[0], adapter_up_matrix[0]], axis=1).astype(bf16)
    all16 = lax.all_gather(both16, "z", axis=0, tiled=True)

    own_counts = counts[0]
    upper = jnp.cumsum(own_counts)
    lower = upper - own_counts
    slot = jnp.arange(NS * ROWS, dtype=jnp.int32)
    slot_owner = (slot % ROWS) // CAP * NS + slot // ROWS
    slot_k = slot % CAP
    pick = holder_assignment[None, :] == slot_owner[:, None]
    start = jnp.sum(jnp.where(pick, lower[None, :], 0), axis=1)
    count = jnp.sum(jnp.where(pick, own_counts[None, :], 0), axis=1)
    source = jnp.where(slot_k < count, start + slot_k, -1)
    route = (source[:, None] == jnp.arange(tok_rows, dtype=jnp.int32)[None, :]).astype(bf16)

    x_send = dot(route, tokens, out=bf16)
    x_rows = lax.all_to_all(x_send, ("x", "c"), 0, 0, tiled=True)
    g_send = dot(route, cotangent, out=bf16)
    g_rows = lax.all_to_all(g_send, ("x", "c"), 0, 0, tiled=True)

    half = feat // NC
    halves = []
    for k in range(1, NT):
        piece = lax.dynamic_slice(
            frozen_key_weight, (((t + k) % NT) * feat + c * half, 0), (half, keyw)
        )
        halves.append(shift(piece, k))
    other = [lax.ppermute(v, "c", [(0, 1), (1, 0)]) for v in halves]
    own_w = lax.dynamic_slice(frozen_key_weight, (t * feat, 0), (feat, keyw))
    weight, base_out, *outs = run_base(c, tokens, own_w, halves, other)
    for k in range(1, NT):
        base_out = base_out + shift(outs[k - 1], -k)
    cots = [cotangent] + [shift(cotangent, k) for k in range(1, NT)]
    base_grad = dot(jnp.concatenate(cots, axis=1), weight, ((1,), (1,)))

    def parts_of(own):
        return [own] + [shift(own, k) for k in range(1, NT)]

    back16, grad_part = run_grad(parts_of(run_back(g_rows, all16, feat, keyw)), x_rows)
    grad_down = lax.psum_scatter(grad_part, "z", scatter_dimension=0, tiled=True)
    adapter_grad = run_adg(back16, all16, feat)
    ret_grad = lax.all_to_all(adapter_grad, ("x", "c"), 0, 0, tiled=True)

    hidden = parts_of(run_hid(x_rows, all16))
    adapter_out, up_part = run_up(hidden, g_rows, all16, feat)
    ret_out = lax.all_to_all(adapter_out, ("x", "c"), 0, 0, tiled=True)
    parts = lax.all_to_all(up_part, "z", 0, 0, tiled=True)
    grad_up = jnp.sum(parts.reshape(NZ, rank, keyw), axis=0)

    layer_out = (base_out + dot(route, ret_out, ((0,), (0,)))).astype(bf16)
    input_grad = (base_grad + dot(route, ret_grad, ((0,), (0,)))).astype(bf16)
    fresh_down = optimizer_update(
        adapter_down_matrix[0], down_first_moment[0], down_second_moment[0], grad_down
    )
    fresh_up = optimizer_update(
        adapter_up_matrix[0], up_first_moment[0], up_second_moment[0], adapter_scale * grad_up
    )
    return (layer_out, input_grad) + tuple(v[None] for v in fresh_down + fresh_up)


def solution(mesh):
    split = Mesh(mesh.devices.reshape(NZ, NX, NC, NT), ("z", "x", "c", "t"))
    dp = ("z", "x", "c")
    act = P(dp, "t")
    state = P(dp, None, "t")
    return jax.shard_map(
        step,
        mesh=split,
        in_specs=(act, act, P(None, "t"), P(dp, None), P()) + (state,) * 6,
        out_specs=(act, act) + (state,) * 6,
        check_vma=False,
    )
```

```python
import jax
import jax.numpy as jnp
from jax import lax
from jax.experimental import pallas as pl
from jax.experimental.pallas import tpu as pltpu
from jax.sharding import Mesh, PartitionSpec as P


adapter_scale = 2.0
learn_rate = 0.01
beta_one = 0.9
beta_two = 0.999
adam_eps = 1e-08
adam_step = 10

NZ, NX, NC, NT = 8, 4, 2, 4
NS = NX * NC
CAP = 12
ROWS = NZ * CAP


bf16 = jnp.bfloat16
f32 = jnp.float32
R = NS * ROWS
MID = R // 2
RANK = 64
PAIR = 2 * RANK
WIDE = NZ * RANK


def optimizer_update(weight, moment, second, grad):
    moment_new = beta_one * moment + (1.0 - beta_one) * grad
    second_new = beta_two * second + (1.0 - beta_two) * grad * grad
    first_fix = 1.0 - beta_one**adam_step
    second_fix = 1.0 - beta_two**adam_step
    weight_new = weight - learn_rate * (moment_new / first_fix) / (
        jnp.sqrt(second_new / second_fix) + adam_eps
    )
    return (weight_new, moment_new, second_new)


def shift(v, k):
    return lax.ppermute(v, "t", [(i, (i + k) % NT) for i in range(NT)])


def dot(a, b, dims=((1,), (0,)), out=f32):
    return lax.dot_general(a, b, (dims, ((), ())), preferred_element_type=out)


def call(body, outs, specs=None, out_specs=None, grid=(), scratch=()):
    vm = pl.BlockSpec(memory_space=pltpu.VMEM)
    kw = {}
    if grid:
        kw["grid"] = grid
    one = not isinstance(outs, (tuple, list))
    return pl.pallas_call(
        body,
        out_shape=outs,
        in_specs=specs,
        out_specs=out_specs or (vm if one else [vm] * len(outs)),
        scratch_shapes=list(scratch),
        **kw,
    )


VM = pl.BlockSpec(memory_space=pltpu.VMEM)


def whole(shape):
    return pl.BlockSpec(shape, lambda *_: (0,) * len(shape))


def row_mask():
    r = lax.broadcasted_iota(jnp.int32, (ROWS, WIDE), 0)
    first = lax.shift_right_logical(lax.broadcasted_iota(jnp.int32, (ROWS, WIDE), 1), 6) * CAP
    return (r >= first) & (r < first + CAP)


def fold(v):
    mask = row_mask()
    rows = []
    for s in range(NS):
        m = jnp.where(mask, v[s * ROWS : (s + 1) * ROWS], 0.0)
        rows.append(sum(m[:, q * PAIR : (q + 1) * PAIR] for q in range(1, NZ // 2)) + m[:, :PAIR])
    half = NS // 2
    return jnp.concatenate(
        [rows[s] + pltpu.roll(rows[s + half], RANK, 1) for s in range(half)], axis=0
    )


def spread_rows(total, out_ref):
    mask = row_mask()
    both = (total, pltpu.roll(total, RANK, 1))
    for s in range(NS):
        half, at = s // (NS // 2), s % (NS // 2) * ROWS
        v = both[half][at : at + ROWS]
        out_ref[pl.ds(s * ROWS, ROWS), :] = jnp.where(
            mask, jnp.concatenate([v] * (NZ // 2), axis=1), 0.0
        ).astype(bf16)


def spread_cols(total, out_ref):
    lo = total.T
    hi = jnp.concatenate([lo[RANK:], lo[:RANK]], axis=0)
    both = jnp.concatenate([lo, hi], axis=1)
    col = lax.broadcasted_iota(jnp.int32, (RANK, R), 1)
    for s in range(1, NS):
        col = jnp.where(lax.broadcasted_iota(jnp.int32, (RANK, R), 1) >= s * ROWS, col - ROWS, col)
    for a in range(NZ):
        keep = (col >= a * CAP) & (col < (a + 1) * CAP)
        v = both[(a % 2) * RANK : (a % 2 + 1) * RANK]
        out_ref[pl.ds(a * RANK, RANK), :] = jnp.where(keep, v, 0.0).astype(bf16)


def back_kernel(g, up, out):
    out[...] = fold(dot(g[...], up[...], ((1,), (1,))))


def grad_kernel(a, b, c, d, x, back16, grad, cols):
    @pl.when(pl.program_id(0) == 0)
    def _():
        total = adapter_scale * (a[...] + b[...] + c[...] + d[...])
        spread_rows(total, back16)
        spread_cols(total, cols)

    grad[...] = dot(cols[...], x[...])


def adg_kernel(back16, down, out):
    out[...] = dot(back16[...], down[...]).astype(bf16)


def hid_kernel(x, down, out, acc):
    @pl.when(pl.program_id(0) == 0)
    def _():
        acc[...] = jnp.zeros_like(acc)

    acc[...] += dot(x[...], down[...], ((1,), (1,)))

    @pl.when(pl.program_id(0) == pl.num_programs(0) - 1)
    def _():
        out[...] = fold(acc[...])


def up_kernel(a, b, c, d, g, up, out, grad, rows, cols):
    total = a[...] + b[...] + c[...] + d[...]
    spread_rows(total, rows)
    spread_cols(total, cols)
    out[...] = (adapter_scale * dot(rows[...], up[...])).astype(bf16)
    grad[...] = dot(cols[...], g[...])


def base_kernel(at, tokens, own, *refs):
    cots, mine, other = refs[:NT], refs[NT : 2 * NT - 1], refs[2 * NT - 1 : 3 * NT - 2]
    grad, parts = refs[3 * NT - 2], refs[3 * NT - 1 :]
    step = pl.program_id(0)

    def half(pieces):
        total = dot(cots[0][...], own[...], ((1,), (1,)))
        for cot, w in zip(cots[1:], pieces):
            total = total + dot(cot[...], w[...], ((1,), (1,)))
        grad[...] = total
        for part, w in zip(parts, (own,) + pieces):
            v = dot(tokens[...], w[...])

            @pl.when(step == 0)
            def _():
                part[...] = v

            @pl.when(step != 0)
            def _():
                part[...] += v

    @pl.when(step == at[0])
    def _():
        half(mine)

    @pl.when(step != at[0])
    def _():
        half(other)


def cast_kernel(down, up, out):
    feat = down.shape[2]
    out[:, :feat] = down[0].astype(bf16)
    out[:, feat:] = up[0].astype(bf16)


def route_kernel(counts, holder, cot, route, out):
    n = counts.shape[1]
    before = lax.broadcasted_iota(jnp.int32, (n, n), 0) < lax.broadcasted_iota(jnp.int32, (n, n), 1)
    rows = jnp.broadcast_to(counts[...].astype(f32), (16, n)).astype(bf16)
    lower = dot(rows, jnp.where(before, 1.0, 0.0).astype(bf16))[:1].astype(jnp.int32)
    code = lower * 16 + counts[...]
    r = lax.broadcasted_iota(jnp.int32, (ROWS, n), 0)
    zi = sum(jnp.where(r >= q * CAP, 1, 0) for q in range(1, NZ))
    k = (r - zi * CAP)[:, :1]
    tok = lax.broadcasted_iota(jnp.int32, (ROWS, route.shape[1]), 1)
    for s in range(NS):
        mine = jnp.sum(jnp.where(holder[...] == zi * NS + s, code, 0), axis=1, keepdims=True)
        src = jnp.where(k < (mine & 15), lax.shift_right_logical(mine, 4) + k, -1)
        route[pl.ds(s * ROWS, ROWS), :] = jnp.where(tok == src, 1.0, 0.0).astype(bf16)
    out[...] = dot(route[...], cot[...]).astype(bf16)


def run_back(g_rows, all16, feat, keyw):
    return call(
        back_kernel,
        jax.ShapeDtypeStruct((MID, PAIR), f32),
        [whole((R, keyw)), pl.BlockSpec((WIDE, keyw), lambda i: (0, feat // keyw))],
        whole((MID, PAIR)),
        (1,),
    )(g_rows, all16)


def run_grad(parts, x_rows):
    feat = x_rows.shape[1]
    nb = 4
    return call(
        grad_kernel,
        [jax.ShapeDtypeStruct((R, WIDE), bf16), jax.ShapeDtypeStruct((WIDE, feat), f32)],
        [whole((MID, PAIR))] * 4 + [pl.BlockSpec((R, feat // nb), lambda j: (0, j))],
        [whole((R, WIDE)), pl.BlockSpec((WIDE, feat // nb), lambda j: (0, j))],
        (nb,),
        [pltpu.VMEM((WIDE, R), bf16)],
    )(*parts, x_rows)


def run_adg(back16, all16, feat):
    nb = 4
    return call(
        adg_kernel,
        jax.ShapeDtypeStruct((R, feat), bf16),
        [whole((R, WIDE)), pl.BlockSpec((WIDE, feat // nb), lambda j: (0, j))],
        pl.BlockSpec((R, feat // nb), lambda j: (0, j)),
        (nb,),
    )(back16, all16)


def run_hid(x_rows, all16):
    feat = x_rows.shape[1]
    nb = 4
    return call(
        hid_kernel,
        jax.ShapeDtypeStruct((MID, PAIR), f32),
        [
            pl.BlockSpec((R, feat // nb), lambda j: (0, j)),
            pl.BlockSpec((WIDE, feat // nb), lambda j: (0, j)),
        ],
        whole((MID, PAIR)),
        (nb,),
        [pltpu.VMEM((R, WIDE), f32)],
    )(x_rows, all16)


def run_up(parts, g_rows, all16, feat):
    keyw = g_rows.shape[1]
    return call(
        up_kernel,
        [jax.ShapeDtypeStruct((R, keyw), bf16), jax.ShapeDtypeStruct((WIDE, keyw), f32)],
        [whole((MID, PAIR))] * 4
        + [whole((R, keyw)), pl.BlockSpec((WIDE, keyw), lambda i: (0, feat // keyw))],
        [whole((R, keyw)), whole((WIDE, keyw))],
        (1,),
        [pltpu.VMEM((R, WIDE), bf16), pltpu.VMEM((WIDE, R), bf16)],
    )(*parts, g_rows, all16)


def run_base(c, t, tokens, weight, cots, mine, other):
    rows, feat = tokens.shape
    keyw = weight.shape[1]
    half = feat // NC
    return pl.pallas_call(
        base_kernel,
        out_shape=[jax.ShapeDtypeStruct((rows, feat), f32)]
        + [jax.ShapeDtypeStruct((rows, keyw), f32)] * NT,
        grid_spec=pltpu.PrefetchScalarGridSpec(
            num_scalar_prefetch=1,
            grid=(NC,),
            in_specs=[
                pl.BlockSpec((rows, half), lambda i, at: (0, i)),
                pl.BlockSpec((half, keyw), lambda i, at: (at[1] * NC + i, 0)),
            ]
            + [whole((rows, keyw))] * NT
            + [whole((half, keyw))] * (2 * NT - 2),
            out_specs=[pl.BlockSpec((rows, half), lambda i, at: (0, i))]
            + [whole((rows, keyw))] * NT,
        ),
        name="base_kernel",
    )(jnp.stack([c, t]), tokens, weight, *cots, *mine, *other)


def step(
    tokens,
    cotangent,
    frozen_key_weight,
    counts,
    holder_assignment,
    adapter_down_matrix,
    adapter_up_matrix,
    down_first_moment,
    down_second_moment,
    up_first_moment,
    up_second_moment,
):
    tok_rows, feat = tokens.shape
    keyw = cotangent.shape[1]
    rank = adapter_down_matrix.shape[1]
    t = lax.axis_index("t")
    c = lax.axis_index("c")
    z = lax.axis_index("z")

    both16 = call(cast_kernel, jax.ShapeDtypeStruct((rank, feat + keyw), bf16), [VM] * 2)(
        adapter_down_matrix, adapter_up_matrix
    )
    all16 = lax.all_gather(both16, "z", axis=0, tiled=True)

    route, g_send = call(
        route_kernel,
        [jax.ShapeDtypeStruct((R, tok_rows), bf16), jax.ShapeDtypeStruct((R, keyw), bf16)],
        [VM] * 3,
    )(counts, holder_assignment.reshape(1, -1), cotangent)
    x_send = dot(route, tokens, out=bf16)
    x_rows = lax.all_to_all(x_send, ("x", "c"), 0, 0, tiled=True)
    g_rows = lax.all_to_all(g_send, ("x", "c"), 0, 0, tiled=True)

    half = feat // NC
    halves = []
    for k in range(1, NT):
        piece = lax.dynamic_slice(
            frozen_key_weight, (((t + k) % NT) * feat + c * half, 0), (half, keyw)
        )
        halves.append(shift(piece, k))
    other = [lax.ppermute(v, "c", [(0, 1), (1, 0)]) for v in halves]
    cots = [cotangent] + [shift(cotangent, k) for k in range(1, NT)]
    base_grad, base_out, *outs = run_base(c, t, tokens, frozen_key_weight, cots, halves, other)
    for k in range(1, NT):
        base_out = base_out + shift(outs[k - 1], -k)

    def parts_of(own):
        return [own] + [shift(own, k) for k in range(1, NT)]

    back16, grad_part = run_grad(parts_of(run_back(g_rows, all16, feat, keyw)), x_rows)
    grad_down = lax.psum_scatter(grad_part, "z", scatter_dimension=0, tiled=True)
    adapter_grad = run_adg(back16, all16, feat)
    ret_grad = lax.all_to_all(adapter_grad, ("x", "c"), 0, 0, tiled=True)

    hidden = parts_of(run_hid(x_rows, all16))
    adapter_out, up_part = run_up(hidden, g_rows, all16, feat)
    ret_out = lax.all_to_all(adapter_out, ("x", "c"), 0, 0, tiled=True)
    grad_up = up_part
    for bit in range(3):
        split = grad_up.reshape(-1, 2, rank, keyw)
        here = lax.shift_right_logical(z, bit) & 1
        keep = lax.dynamic_index_in_dim(split, here, 1, keepdims=False)
        give = lax.dynamic_index_in_dim(split, 1 - here, 1, keepdims=False)
        grad_up = keep + lax.ppermute(give, "z", [(i, i ^ (1 << bit)) for i in range(NZ)])
    grad_up = grad_up.reshape(rank, keyw)

    layer_out = (base_out + dot(route, ret_out, ((0,), (0,)))).astype(bf16)
    input_grad = (base_grad + dot(route, ret_grad, ((0,), (0,)))).astype(bf16)
    fresh_down = optimizer_update(
        adapter_down_matrix[0], down_first_moment[0], down_second_moment[0], grad_down
    )
    fresh_up = optimizer_update(
        adapter_up_matrix[0], up_first_moment[0], up_second_moment[0], adapter_scale * grad_up
    )
    return (layer_out, input_grad) + tuple(v[None] for v in fresh_down + fresh_up)


def solution(mesh):
    split = Mesh(mesh.devices.reshape(NZ, NX, NC, NT), ("z", "x", "c", "t"))
    dp = ("z", "x", "c")
    act = P(dp, "t")
    state = P(dp, None, "t")
    return jax.shard_map(
        step,
        mesh=split,
        in_specs=(act, act, P(None, "t"), P(dp, None), P()) + (state,) * 6,
        out_specs=(act, act) + (state,) * 6,
        check_vma=False,
    )
```

```python
import jax
import jax.numpy as jnp
from jax import lax
from jax.experimental import pallas as pl
from jax.experimental.pallas import tpu as pltpu
from jax.sharding import Mesh, PartitionSpec as P


adapter_scale = 2.0
learn_rate = 0.01
beta_one = 0.9
beta_two = 0.999
adam_eps = 1e-08
adam_step = 10

NZ, NX, NC, NT = 8, 4, 2, 4
NS = NX * NC
CAP = 12
ROWS = NZ * CAP


bf16 = jnp.bfloat16
f32 = jnp.float32
R = NS * ROWS
MID = R // 2
RANK = 64
PAIR = 2 * RANK
WIDE = NZ * RANK


def optimizer_update(weight, moment, second, grad):
    moment_new = beta_one * moment + (1.0 - beta_one) * grad
    second_new = beta_two * second + (1.0 - beta_two) * grad * grad
    first_fix = 1.0 - beta_one**adam_step
    second_fix = 1.0 - beta_two**adam_step
    weight_new = weight - learn_rate * (moment_new / first_fix) / (
        jnp.sqrt(second_new / second_fix) + adam_eps
    )
    return (weight_new, moment_new, second_new)


def shift(v, k):
    return lax.ppermute(v, "t", [(i, (i + k) % NT) for i in range(NT)])


def dot(a, b, dims=((1,), (0,)), out=f32):
    return lax.dot_general(a, b, (dims, ((), ())), preferred_element_type=out)


def call(body, outs, specs=None, out_specs=None, grid=(), scratch=()):
    vm = pl.BlockSpec(memory_space=pltpu.VMEM)
    kw = {}
    if grid:
        kw["grid"] = grid
    one = not isinstance(outs, (tuple, list))
    return pl.pallas_call(
        body,
        out_shape=outs,
        in_specs=specs,
        out_specs=out_specs or (vm if one else [vm] * len(outs)),
        scratch_shapes=list(scratch),
        **kw,
    )


VM = pl.BlockSpec(memory_space=pltpu.VMEM)


def whole(shape):
    return pl.BlockSpec(shape, lambda *_: (0,) * len(shape))


def row_mask():
    r = lax.broadcasted_iota(jnp.int32, (ROWS, WIDE), 0)
    first = lax.shift_right_logical(lax.broadcasted_iota(jnp.int32, (ROWS, WIDE), 1), 6) * CAP
    return (r >= first) & (r < first + CAP)


def fold(v):
    mask = row_mask()
    rows = []
    for s in range(NS):
        m = jnp.where(mask, v[s * ROWS : (s + 1) * ROWS], 0.0)
        rows.append(sum(m[:, q * PAIR : (q + 1) * PAIR] for q in range(1, NZ // 2)) + m[:, :PAIR])
    half = NS // 2
    return jnp.concatenate(
        [rows[s] + pltpu.roll(rows[s + half], RANK, 1) for s in range(half)], axis=0
    )


def spread_rows(total, out_ref):
    mask = row_mask()
    both = (total, pltpu.roll(total, RANK, 1))
    for s in range(NS):
        half, at = s // (NS // 2), s % (NS // 2) * ROWS
        v = both[half][at : at + ROWS]
        out_ref[pl.ds(s * ROWS, ROWS), :] = jnp.where(
            mask, jnp.concatenate([v] * (NZ // 2), axis=1), 0.0
        ).astype(bf16)


def spread_cols(total, out_ref):
    lo = total.T
    hi = jnp.concatenate([lo[RANK:], lo[:RANK]], axis=0)
    both = jnp.concatenate([lo, hi], axis=1)
    col = lax.broadcasted_iota(jnp.int32, (RANK, R), 1)
    for s in range(1, NS):
        col = jnp.where(lax.broadcasted_iota(jnp.int32, (RANK, R), 1) >= s * ROWS, col - ROWS, col)
    for a in range(NZ):
        keep = (col >= a * CAP) & (col < (a + 1) * CAP)
        v = both[(a % 2) * RANK : (a % 2 + 1) * RANK]
        out_ref[pl.ds(a * RANK, RANK), :] = jnp.where(keep, v, 0.0).astype(bf16)


def back_kernel(g, up, out):
    out[...] = fold(dot(g[...], up[...], ((1,), (1,))))


def grad_kernel(a, b, c, d, x, back16, grad, cols):
    @pl.when(pl.program_id(0) == 0)
    def _():
        total = adapter_scale * (a[...] + b[...] + c[...] + d[...])
        spread_rows(total, back16)
        spread_cols(total, cols)

    grad[...] = dot(cols[...], x[...])


def adg_kernel(back16, first, second, out):
    @pl.when(pl.program_id(0) == 0)
    def _():
        out[...] = dot(back16[...], first[...]).astype(bf16)

    @pl.when(pl.program_id(0) == 1)
    def _():
        out[...] = dot(back16[...], second[...]).astype(bf16)


def hid_kernel(x, first, second, out, acc):
    @pl.when(pl.program_id(0) == 0)
    def _():
        acc[...] = dot(x[...], first[...], ((1,), (1,)))

    @pl.when(pl.program_id(0) == 1)
    def _():
        out[...] = fold(acc[...] + dot(x[...], second[...], ((1,), (1,))))


def up_kernel(a, b, c, d, g, up, out, grad, rows, cols):
    total = a[...] + b[...] + c[...] + d[...]
    spread_rows(total, rows)
    spread_cols(total, cols)
    out[...] = (adapter_scale * dot(rows[...], up[...])).astype(bf16)
    grad[...] = dot(cols[...], g[...])


def base_kernel(at, tokens, own, *refs):
    cots, mine, other = refs[:NT], refs[NT : 2 * NT - 1], refs[2 * NT - 1 : 3 * NT - 2]
    grad, parts = refs[3 * NT - 2], refs[3 * NT - 1 :]
    step = pl.program_id(0)

    def half(pieces):
        total = dot(cots[0][...], own[...], ((1,), (1,)))
        for cot, w in zip(cots[1:], pieces):
            total = total + dot(cot[...], w[...], ((1,), (1,)))
        grad[...] = total
        for part, w in zip(parts, (own,) + pieces):
            v = dot(tokens[...], w[...])

            @pl.when(step == 0)
            def _():
                part[...] = v

            @pl.when(step != 0)
            def _():
                part[...] += v

    @pl.when(step == at[0])
    def _():
        half(mine)

    @pl.when(step != at[0])
    def _():
        half(other)


def cast_kernel(down, up, first, second):
    half = second.shape[1]
    first[:, :half] = down[0, :, :half].astype(bf16)
    first[:, half:] = up[0].astype(bf16)
    second[...] = down[0, :, half:].astype(bf16)


def place_kernel(me, *refs):
    out = refs[-1]
    for k, ref in enumerate(refs[:-1]):
        at = pl.multiple_of(lax.rem(me[0] + NS - k, NS) * ROWS, ROWS)
        out[pl.ds(at, ROWS), :] = ref[...]


def route_kernel(counts, holder, cot, route, out):
    n = counts.shape[1]
    before = lax.broadcasted_iota(jnp.int32, (n, n), 0) < lax.broadcasted_iota(jnp.int32, (n, n), 1)
    rows = jnp.broadcast_to(counts[...].astype(f32), (16, n)).astype(bf16)
    lower = dot(rows, jnp.where(before, 1.0, 0.0).astype(bf16))[:1].astype(jnp.int32)
    code = lower * 16 + counts[...]
    r = lax.broadcasted_iota(jnp.int32, (ROWS, n), 0)
    zi = sum(jnp.where(r >= q * CAP, 1, 0) for q in range(1, NZ))
    k = (r - zi * CAP)[:, :1]
    tok = lax.broadcasted_iota(jnp.int32, (ROWS, route.shape[1]), 1)
    for s in range(NS):
        mine = jnp.sum(jnp.where(holder[...] == zi * NS + s, code, 0), axis=1, keepdims=True)
        src = jnp.where(k < (mine & 15), lax.shift_right_logical(mine, 4) + k, -1)
        route[pl.ds(s * ROWS, ROWS), :] = jnp.where(tok == src, 1.0, 0.0).astype(bf16)
    out[...] = dot(route[...], cot[...]).astype(bf16)


def run_back(g_rows, first):
    keyw = g_rows.shape[1]
    at = first.shape[1] // keyw - 1
    return call(
        back_kernel,
        jax.ShapeDtypeStruct((MID, PAIR), f32),
        [whole((R, keyw)), pl.BlockSpec((WIDE, keyw), lambda i: (0, at))],
        whole((MID, PAIR)),
        (1,),
    )(g_rows, first)


def run_grad(parts, x_rows):
    half = x_rows.shape[1] // 2
    return call(
        grad_kernel,
        [jax.ShapeDtypeStruct((R, WIDE), bf16), jax.ShapeDtypeStruct((WIDE, 2 * half), f32)],
        [whole((MID, PAIR))] * 4 + [pl.BlockSpec((R, half), lambda j: (0, j))],
        [whole((R, WIDE)), pl.BlockSpec((WIDE, half), lambda j: (0, j))],
        (2,),
        [pltpu.VMEM((WIDE, R), bf16)],
    )(*parts, x_rows)


def run_adg(back16, first, second):
    half = second.shape[1]
    return call(
        adg_kernel,
        jax.ShapeDtypeStruct((R, 2 * half), bf16),
        [whole((R, WIDE)), whole((WIDE, half)), whole((WIDE, half))],
        pl.BlockSpec((R, half), lambda j: (0, j)),
        (2,),
    )(back16, first, second)


def run_hid(x_rows, first, second):
    half = second.shape[1]
    return call(
        hid_kernel,
        jax.ShapeDtypeStruct((MID, PAIR), f32),
        [pl.BlockSpec((R, half), lambda j: (0, j)), whole((WIDE, half)), whole((WIDE, half))],
        whole((MID, PAIR)),
        (2,),
        [pltpu.VMEM((R, WIDE), f32)],
    )(x_rows, first, second)


def run_up(parts, g_rows, first):
    keyw = g_rows.shape[1]
    at = first.shape[1] // keyw - 1
    return call(
        up_kernel,
        [jax.ShapeDtypeStruct((R, keyw), bf16), jax.ShapeDtypeStruct((WIDE, keyw), f32)],
        [whole((MID, PAIR))] * 4
        + [whole((R, keyw)), pl.BlockSpec((WIDE, keyw), lambda i: (0, at))],
        [whole((R, keyw)), whole((WIDE, keyw))],
        (1,),
        [pltpu.VMEM((R, WIDE), bf16), pltpu.VMEM((WIDE, R), bf16)],
    )(*parts, g_rows, first)


def run_base(c, t, tokens, weight, cots, mine, other):
    rows, feat = tokens.shape
    keyw = weight.shape[1]
    half = feat // NC
    return pl.pallas_call(
        base_kernel,
        out_shape=[jax.ShapeDtypeStruct((rows, feat), f32)]
        + [jax.ShapeDtypeStruct((rows, keyw), f32)] * NT,
        grid_spec=pltpu.PrefetchScalarGridSpec(
            num_scalar_prefetch=1,
            grid=(NC,),
            in_specs=[
                pl.BlockSpec((rows, half), lambda i, at: (0, i)),
                pl.BlockSpec((half, keyw), lambda i, at: (at[1] * NC + i, 0)),
            ]
            + [whole((rows, keyw))] * NT
            + [whole((half, keyw))] * (2 * NT - 2),
            out_specs=[pl.BlockSpec((rows, half), lambda i, at: (0, i))]
            + [whole((rows, keyw))] * NT,
        ),
        name="base_kernel",
    )(jnp.stack([c, t]), tokens, weight, *cots, *mine, *other)


def step(
    tokens,
    cotangent,
    frozen_key_weight,
    counts,
    holder_assignment,
    adapter_down_matrix,
    adapter_up_matrix,
    down_first_moment,
    down_second_moment,
    up_first_moment,
    up_second_moment,
):
    tok_rows, feat = tokens.shape
    keyw = cotangent.shape[1]
    rank = adapter_down_matrix.shape[1]
    t = lax.axis_index("t")
    c = lax.axis_index("c")
    z = lax.axis_index("z")
    xc = lax.axis_index(("x", "c"))

    first16, second16 = call(
        cast_kernel,
        [
            jax.ShapeDtypeStruct((rank, feat // 2 + keyw), bf16),
            jax.ShapeDtypeStruct((rank, feat // 2), bf16),
        ],
        [VM] * 2,
    )(adapter_down_matrix, adapter_up_matrix)
    first = lax.all_gather(first16, "z", axis=0, tiled=True)
    second = lax.all_gather(second16, "z", axis=0, tiled=True)

    route, g_send = call(
        route_kernel,
        [jax.ShapeDtypeStruct((R, tok_rows), bf16), jax.ShapeDtypeStruct((R, keyw), bf16)],
        [VM] * 3,
    )(counts, holder_assignment.reshape(1, -1), cotangent)
    x_send = dot(route, tokens, out=bf16)
    x_rows = lax.all_to_all(x_send, ("x", "c"), 0, 0, tiled=True)
    g_rows = lax.all_to_all(g_send, ("x", "c"), 0, 0, tiled=True)

    half = feat // NC
    halves = []
    for k in range(1, NT):
        piece = lax.dynamic_slice(
            frozen_key_weight, (((t + k) % NT) * feat + c * half, 0), (half, keyw)
        )
        halves.append(shift(piece, k))
    other = [lax.ppermute(v, "c", [(0, 1), (1, 0)]) for v in halves]
    cots = [cotangent] + [shift(cotangent, k) for k in range(1, NT)]
    base_grad, base_out, *outs = run_base(c, t, tokens, frozen_key_weight, cots, halves, other)
    for k in range(1, NT):
        base_out = base_out + shift(outs[k - 1], -k)

    def parts_of(own):
        return [own] + [shift(own, k) for k in range(1, NT)]

    back16, grad_part = run_grad(parts_of(run_back(g_rows, first)), x_rows)
    grad_down = lax.psum_scatter(grad_part, "z", scatter_dimension=0, tiled=True)
    adapter_grad = run_adg(back16, first, second)
    ret_grad = lax.all_to_all(adapter_grad, ("x", "c"), 0, 0, tiled=True)

    hidden = parts_of(run_hid(x_rows, first, second))
    adapter_out, up_part = run_up(hidden, g_rows, first)
    chunks = [
        lax.dynamic_slice(adapter_out, ((xc + k) % NS * ROWS, 0), (ROWS, keyw))
        for k in range(NS)
    ]
    chunks[1:] = [
        lax.ppermute(v, ("x", "c"), [(i, (i + k) % NS) for i in range(NS)])
        for k, v in enumerate(chunks[1:], 1)
    ]
    ret_out = call(
        place_kernel,
        jax.ShapeDtypeStruct((R, keyw), bf16),
        [pl.BlockSpec(memory_space=pltpu.SMEM)] + [VM] * NS,
    )(xc.reshape(1), *chunks)
    grad_up = up_part
    for bit in range(3):
        split = grad_up.reshape(-1, 2, rank, keyw)
        here = lax.shift_right_logical(z, bit) & 1
        keep = lax.dynamic_index_in_dim(split, here, 1, keepdims=False)
        give = lax.dynamic_index_in_dim(split, 1 - here, 1, keepdims=False)
        grad_up = keep + lax.ppermute(give, "z", [(i, i ^ (1 << bit)) for i in range(NZ)])
    grad_up = grad_up.reshape(rank, keyw)

    layer_out = (base_out + dot(route, ret_out, ((0,), (0,)))).astype(bf16)
    input_grad = (base_grad + dot(route, ret_grad, ((0,), (0,)))).astype(bf16)
    fresh_down = optimizer_update(
        adapter_down_matrix[0], down_first_moment[0], down_second_moment[0], grad_down
    )
    fresh_up = optimizer_update(
        adapter_up_matrix[0], up_first_moment[0], up_second_moment[0], adapter_scale * grad_up
    )
    return (layer_out, input_grad) + tuple(v[None] for v in fresh_down + fresh_up)


def solution(mesh):
    split = Mesh(mesh.devices.reshape(NZ, NX, NC, NT), ("z", "x", "c", "t"))
    dp = ("z", "x", "c")
    act = P(dp, "t")
    state = P(dp, None, "t")
    return jax.shard_map(
        step,
        mesh=split,
        in_specs=(act, act, P(None, "t"), P(dp, None), P()) + (state,) * 6,
        out_specs=(act, act) + (state,) * 6,
        check_vma=False,
    )
```

```python
import jax
import jax.numpy as jnp
from jax import lax
from jax.experimental import pallas as pl
from jax.experimental.pallas import tpu as pltpu
from jax.sharding import Mesh, PartitionSpec as P


adapter_scale = 2.0
learn_rate = 0.01
beta_one = 0.9
beta_two = 0.999
adam_eps = 1e-08
adam_step = 10

NZ, NX, NC, NT = 8, 4, 2, 4
NS = NX * NC
CAP = 12
ROWS = NZ * CAP


bf16 = jnp.bfloat16
f32 = jnp.float32
R = NS * ROWS
MID = R // 2
RANK = 64
PAIR = 2 * RANK
WIDE = NZ * RANK


def optimizer_update(weight, moment, second, grad):
    moment_new = beta_one * moment + (1.0 - beta_one) * grad
    second_new = beta_two * second + (1.0 - beta_two) * grad * grad
    first_fix = 1.0 - beta_one**adam_step
    second_fix = 1.0 - beta_two**adam_step
    weight_new = weight - learn_rate * (moment_new / first_fix) / (
        jnp.sqrt(second_new / second_fix) + adam_eps
    )
    return (weight_new, moment_new, second_new)


def shift(v, k):
    return lax.ppermute(v, "t", [(i, (i + k) % NT) for i in range(NT)])


def dot(a, b, dims=((1,), (0,)), out=f32):
    return lax.dot_general(a, b, (dims, ((), ())), preferred_element_type=out)


def call(body, outs, specs=None, out_specs=None, grid=(), scratch=()):
    vm = pl.BlockSpec(memory_space=pltpu.VMEM)
    kw = {}
    if grid:
        kw["grid"] = grid
    one = not isinstance(outs, (tuple, list))
    return pl.pallas_call(
        body,
        out_shape=outs,
        in_specs=specs,
        out_specs=out_specs or (vm if one else [vm] * len(outs)),
        scratch_shapes=list(scratch),
        **kw,
    )


VM = pl.BlockSpec(memory_space=pltpu.VMEM)


def whole(shape):
    return pl.BlockSpec(shape, lambda *_: (0,) * len(shape))


def row_mask():
    r = lax.broadcasted_iota(jnp.int32, (ROWS, WIDE), 0)
    first = lax.shift_right_logical(lax.broadcasted_iota(jnp.int32, (ROWS, WIDE), 1), 6) * CAP
    return (r >= first) & (r < first + CAP)


def fold(v):
    mask = row_mask()
    rows = []
    for s in range(NS):
        m = jnp.where(mask, v[s * ROWS : (s + 1) * ROWS], 0.0)
        rows.append(sum(m[:, q * PAIR : (q + 1) * PAIR] for q in range(1, NZ // 2)) + m[:, :PAIR])
    half = NS // 2
    return jnp.concatenate(
        [rows[s] + pltpu.roll(rows[s + half], RANK, 1) for s in range(half)], axis=0
    )


def spread_rows(total, out_ref):
    mask = row_mask()
    both = (total, pltpu.roll(total, RANK, 1))
    for s in range(NS):
        half, at = s // (NS // 2), s % (NS // 2) * ROWS
        v = both[half][at : at + ROWS]
        out_ref[pl.ds(s * ROWS, ROWS), :] = jnp.where(
            mask, jnp.concatenate([v] * (NZ // 2), axis=1), 0.0
        ).astype(bf16)


def spread_cols(total, out_ref):
    lo = total.T
    hi = jnp.concatenate([lo[RANK:], lo[:RANK]], axis=0)
    both = jnp.concatenate([lo, hi], axis=1)
    col = lax.broadcasted_iota(jnp.int32, (RANK, R), 1)
    for s in range(1, NS):
        col = jnp.where(lax.broadcasted_iota(jnp.int32, (RANK, R), 1) >= s * ROWS, col - ROWS, col)
    for a in range(NZ):
        keep = (col >= a * CAP) & (col < (a + 1) * CAP)
        v = both[(a % 2) * RANK : (a % 2 + 1) * RANK]
        out_ref[pl.ds(a * RANK, RANK), :] = jnp.where(keep, v, 0.0).astype(bf16)


def back_kernel(g, up, out):
    out[...] = fold(dot(g[...], up[...], ((1,), (1,))))


def grad_kernel(a, b, c, d, x, back16, grad, cols):
    @pl.when(pl.program_id(0) == 0)
    def _():
        total = adapter_scale * (a[...] + b[...] + c[...] + d[...])
        spread_rows(total, back16)
        spread_cols(total, cols)

    grad[...] = dot(cols[...], x[...])


def adg_kernel(back16, down, out):
    out[...] = dot(back16[...], down[...]).astype(bf16)


def hid_kernel(x, down, out, acc):
    @pl.when(pl.program_id(0) == 0)
    def _():
        acc[...] = jnp.zeros_like(acc)

    acc[...] += dot(x[...], down[...], ((1,), (1,)))

    @pl.when(pl.program_id(0) == pl.num_programs(0) - 1)
    def _():
        out[...] = fold(acc[...])


def up_kernel(a, b, c, d, g, up, out, grad, rows, cols):
    total = a[...] + b[...] + c[...] + d[...]
    spread_rows(total, rows)
    spread_cols(total, cols)
    out[...] = (adapter_scale * dot(rows[...], up[...])).astype(bf16)
    grad[...] = dot(cols[...], g[...])


def base_grad_kernel(at, own, *refs):
    cots, mine, other, grad = refs[:NT], refs[NT : 2 * NT - 1], refs[2 * NT - 1 : -1], refs[-1]
    step = pl.program_id(0)

    def half(pieces):
        total = dot(cots[0][...], own[...], ((1,), (1,)))
        for cot, w in zip(cots[1:], pieces):
            total = total + dot(cot[...], w[...], ((1,), (1,)))
        grad[...] = total

    @pl.when(step == at[0])
    def _():
        half(mine)

    @pl.when(step != at[0])
    def _():
        half(other)


def base_out_kernel(at, tokens, own, *refs):
    mine, other, parts = refs[: NT - 1], refs[NT - 1 : 2 * NT - 2], refs[2 * NT - 2 :]
    step = pl.program_id(0)

    def half(pieces):
        for p, w in zip(parts, (own,) + pieces):
            v = dot(tokens[...], w[...])

            @pl.when(step == 0)
            def _():
                p[...] = v

            @pl.when(step != 0)
            def _():
                p[...] += v

    @pl.when(step == at[0])
    def _():
        half(mine)

    @pl.when(step != at[0])
    def _():
        half(other)


def final_kernel(route, ret, base, out):
    out[...] = (base[...] + dot(route[...], ret[...], ((0,), (0,)))).astype(bf16)


def cast_kernel(down, up, out):
    feat = down.shape[2]
    out[:, :feat] = down[0].astype(bf16)
    out[:, feat:] = up[0].astype(bf16)


def route_kernel(counts, holder, cot, route, out):
    n = counts.shape[1]
    before = lax.broadcasted_iota(jnp.int32, (n, n), 0) < lax.broadcasted_iota(jnp.int32, (n, n), 1)
    rows = jnp.broadcast_to(counts[...].astype(f32), (16, n)).astype(bf16)
    lower = dot(rows, jnp.where(before, 1.0, 0.0).astype(bf16))[:1].astype(jnp.int32)
    code = lower * 16 + counts[...]
    r = lax.broadcasted_iota(jnp.int32, (ROWS, n), 0)
    zi = sum(jnp.where(r >= q * CAP, 1, 0) for q in range(1, NZ))
    k = (r - zi * CAP)[:, :1]
    tok = lax.broadcasted_iota(jnp.int32, (ROWS, route.shape[1]), 1)
    for s in range(NS):
        mine = jnp.sum(jnp.where(holder[...] == zi * NS + s, code, 0), axis=1, keepdims=True)
        src = jnp.where(k < (mine & 15), lax.shift_right_logical(mine, 4) + k, -1)
        route[pl.ds(s * ROWS, ROWS), :] = jnp.where(tok == src, 1.0, 0.0).astype(bf16)
    out[...] = dot(route[...], cot[...]).astype(bf16)


def run_back(g_rows, all16, feat, keyw):
    return call(
        back_kernel,
        jax.ShapeDtypeStruct((MID, PAIR), f32),
        [whole((R, keyw)), pl.BlockSpec((WIDE, keyw), lambda i: (0, feat // keyw))],
        whole((MID, PAIR)),
        (1,),
    )(g_rows, all16)


def run_grad(parts, x_rows):
    feat = x_rows.shape[1]
    nb = 2
    return call(
        grad_kernel,
        [jax.ShapeDtypeStruct((R, WIDE), bf16), jax.ShapeDtypeStruct((WIDE, feat), f32)],
        [whole((MID, PAIR))] * 4 + [pl.BlockSpec((R, feat // nb), lambda j: (0, j))],
        [whole((R, WIDE)), pl.BlockSpec((WIDE, feat // nb), lambda j: (0, j))],
        (nb,),
        [pltpu.VMEM((WIDE, R), bf16)],
    )(*parts, x_rows)


def run_adg(back16, all16, feat):
    nb = 2
    return call(
        adg_kernel,
        jax.ShapeDtypeStruct((R, feat), bf16),
        [whole((R, WIDE)), pl.BlockSpec((WIDE, feat // nb), lambda j: (0, j))],
        pl.BlockSpec((R, feat // nb), lambda j: (0, j)),
        (nb,),
    )(back16, all16)


def run_hid(x_rows, all16):
    feat = x_rows.shape[1]
    nb = 2
    return call(
        hid_kernel,
        jax.ShapeDtypeStruct((MID, PAIR), f32),
        [
            pl.BlockSpec((R, feat // nb), lambda j: (0, j)),
            pl.BlockSpec((WIDE, feat // nb), lambda j: (0, j)),
        ],
        whole((MID, PAIR)),
        (nb,),
        [pltpu.VMEM((R, WIDE), f32)],
    )(x_rows, all16)


def run_up(parts, g_rows, all16, feat):
    keyw = g_rows.shape[1]
    return call(
        up_kernel,
        [jax.ShapeDtypeStruct((R, keyw), bf16), jax.ShapeDtypeStruct((WIDE, keyw), f32)],
        [whole((MID, PAIR))] * 4
        + [whole((R, keyw)), pl.BlockSpec((WIDE, keyw), lambda i: (0, feat // keyw))],
        [whole((R, keyw)), whole((WIDE, keyw))],
        (1,),
        [pltpu.VMEM((R, WIDE), bf16), pltpu.VMEM((WIDE, R), bf16)],
    )(*parts, g_rows, all16)


def run_base(kernel, at, lead, lead_specs, weight, pieces, outs, out_specs):
    keyw = weight.shape[1]
    half = pieces[0].shape[0]
    own = pl.BlockSpec((half, keyw), lambda i, at: (at[1] * NC + i, 0))
    n = len(pieces)
    first = kernel is base_out_kernel
    return pl.pallas_call(
        kernel,
        out_shape=outs,
        grid_spec=pltpu.PrefetchScalarGridSpec(
            num_scalar_prefetch=1,
            grid=(NC,),
            in_specs=(lead_specs + [own] if first else [own] + lead_specs)
            + [whole((half, keyw))] * n,
            out_specs=out_specs,
        ),
    )(at, *(lead + [weight] if first else [weight] + lead), *pieces)


def run_base_grad(at, weight, cots, pieces):
    rows, keyw = cots[0].shape
    half = pieces[0].shape[0]
    return run_base(
        base_grad_kernel,
        at,
        cots,
        [whole((rows, keyw))] * NT,
        weight,
        pieces,
        jax.ShapeDtypeStruct((rows, NC * half), f32),
        pl.BlockSpec((rows, half), lambda i, at: (0, i)),
    )


def run_base_out(at, weight, tokens, pieces):
    rows = tokens.shape[0]
    half, keyw = pieces[0].shape
    return run_base(
        base_out_kernel,
        at,
        [tokens],
        [pl.BlockSpec((rows, half), lambda i, at: (0, i))],
        weight,
        pieces,
        [jax.ShapeDtypeStruct((rows, keyw), f32)] * NT,
        [whole((rows, keyw))] * NT,
    )


def run_final(route, ret, base):
    rows, feat = base.shape
    half = feat // 2
    return call(
        final_kernel,
        jax.ShapeDtypeStruct((rows, feat), bf16),
        [whole(route.shape)]
        + [pl.BlockSpec((n, half), lambda j: (0, j)) for n in (ret.shape[0], rows)],
        pl.BlockSpec((rows, half), lambda j: (0, j)),
        (2,),
    )(route, ret, base)


def step(
    tokens,
    cotangent,
    frozen_key_weight,
    counts,
    holder_assignment,
    adapter_down_matrix,
    adapter_up_matrix,
    down_first_moment,
    down_second_moment,
    up_first_moment,
    up_second_moment,
):
    tok_rows, feat = tokens.shape
    keyw = cotangent.shape[1]
    rank = adapter_down_matrix.shape[1]
    t = lax.axis_index("t")
    c = lax.axis_index("c")
    z = lax.axis_index("z")

    both16 = call(cast_kernel, jax.ShapeDtypeStruct((rank, feat + keyw), bf16), [VM] * 2)(
        adapter_down_matrix, adapter_up_matrix
    )
    all16 = lax.all_gather(both16, "z", axis=0, tiled=True)

    route, g_send = call(
        route_kernel,
        [jax.ShapeDtypeStruct((R, tok_rows), bf16), jax.ShapeDtypeStruct((R, keyw), bf16)],
        [VM] * 3,
    )(counts, holder_assignment.reshape(1, -1), cotangent)
    x_send = dot(route, tokens, out=bf16)
    x_rows = lax.all_to_all(x_send, ("x", "c"), 0, 0, tiled=True)
    g_rows = lax.all_to_all(g_send, ("x", "c"), 0, 0, tiled=True)

    half = feat // NC
    halves = []
    for k in range(1, NT):
        piece = lax.dynamic_slice(
            frozen_key_weight, (((t + k) % NT) * feat + c * half, 0), (half, keyw)
        )
        halves.append(shift(piece, k))
    other = [lax.ppermute(v, "c", [(0, 1), (1, 0)]) for v in halves]
    cots = [cotangent] + [shift(cotangent, k) for k in range(1, NT)]
    at = jnp.stack([c, t])
    pieces = halves + other
    base_grad = run_base_grad(at, frozen_key_weight, cots, pieces)
    base_out, *outs = run_base_out(at, frozen_key_weight, tokens, pieces)
    for k in range(1, NT):
        base_out = base_out + shift(outs[k - 1], -k)

    def parts_of(own):
        return [own] + [shift(own, k) for k in range(1, NT)]

    back16, grad_part = run_grad(parts_of(run_back(g_rows, all16, feat, keyw)), x_rows)
    grad_down = lax.psum_scatter(grad_part, "z", scatter_dimension=0, tiled=True)
    adapter_grad = run_adg(back16, all16, feat)
    ret_grad = lax.all_to_all(adapter_grad, ("x", "c"), 0, 0, tiled=True)

    hidden = parts_of(run_hid(x_rows, all16))
    adapter_out, up_part = run_up(hidden, g_rows, all16, feat)
    ret_out = lax.all_to_all(adapter_out, ("x", "c"), 0, 0, tiled=True)
    grad_up = up_part
    for bit in range(3):
        split = grad_up.reshape(-1, 2, rank, keyw)
        here = lax.shift_right_logical(z, bit) & 1
        keep = lax.dynamic_index_in_dim(split, here, 1, keepdims=False)
        give = lax.dynamic_index_in_dim(split, 1 - here, 1, keepdims=False)
        grad_up = keep + lax.ppermute(give, "z", [(i, i ^ (1 << bit)) for i in range(NZ)])
    grad_up = grad_up.reshape(rank, keyw)

    layer_out = (base_out + dot(route, ret_out, ((0,), (0,)))).astype(bf16)
    input_grad = run_final(route, ret_grad, base_grad)
    fresh_down = optimizer_update(
        adapter_down_matrix[0], down_first_moment[0], down_second_moment[0], grad_down
    )
    fresh_up = optimizer_update(
        adapter_up_matrix[0], up_first_moment[0], up_second_moment[0], adapter_scale * grad_up
    )
    return (layer_out, input_grad) + tuple(v[None] for v in fresh_down + fresh_up)


def solution(mesh):
    split = Mesh(mesh.devices.reshape(NZ, NX, NC, NT), ("z", "x", "c", "t"))
    dp = ("z", "x", "c")
    act = P(dp, "t")
    state = P(dp, None, "t")
    return jax.shard_map(
        step,
        mesh=split,
        in_specs=(act, act, P(None, "t"), P(dp, None), P()) + (state,) * 6,
        out_specs=(act, act) + (state,) * 6,
        check_vma=False,
    )
```

```python
import jax
import jax.numpy as jnp
from jax import lax
from jax.experimental import pallas as pl
from jax.experimental.pallas import tpu as pltpu
from jax.sharding import Mesh, PartitionSpec as P


adapter_scale = 2.0
learn_rate = 0.01
beta_one = 0.9
beta_two = 0.999
adam_eps = 1e-08
adam_step = 10

NZ, NX, NC, NT = 8, 4, 2, 4
NS = NX * NC
CAP = 12
ROWS = NZ * CAP


bf16 = jnp.bfloat16
f32 = jnp.float32
R = NS * ROWS
MID = R // 2
RANK = 64
PAIR = 2 * RANK
WIDE = NZ * RANK


def optimizer_update(weight, moment, second, grad):
    moment_new = beta_one * moment + (1.0 - beta_one) * grad
    second_new = beta_two * second + (1.0 - beta_two) * grad * grad
    first_fix = 1.0 - beta_one**adam_step
    second_fix = 1.0 - beta_two**adam_step
    weight_new = weight - learn_rate * (moment_new / first_fix) / (
        jnp.sqrt(second_new / second_fix) + adam_eps
    )
    return (weight_new, moment_new, second_new)


def shift(v, k):
    return lax.ppermute(v, "t", [(i, (i + k) % NT) for i in range(NT)])


def dot(a, b, dims=((1,), (0,)), out=f32):
    return lax.dot_general(a, b, (dims, ((), ())), preferred_element_type=out)


def call(body, outs, specs=None, out_specs=None, grid=(), scratch=()):
    vm = pl.BlockSpec(memory_space=pltpu.VMEM)
    kw = {}
    if grid:
        kw["grid"] = grid
    one = not isinstance(outs, (tuple, list))
    return pl.pallas_call(
        body,
        out_shape=outs,
        in_specs=specs,
        out_specs=out_specs or (vm if one else [vm] * len(outs)),
        scratch_shapes=list(scratch),
        **kw,
    )


VM = pl.BlockSpec(memory_space=pltpu.VMEM)


def whole(shape):
    return pl.BlockSpec(shape, lambda *_: (0,) * len(shape))


def row_mask():
    r = lax.broadcasted_iota(jnp.int32, (ROWS, WIDE), 0)
    first = lax.shift_right_logical(lax.broadcasted_iota(jnp.int32, (ROWS, WIDE), 1), 6) * CAP
    return (r >= first) & (r < first + CAP)


def fold(v):
    mask = row_mask()
    rows = []
    for s in range(NS):
        m = jnp.where(mask, v[s * ROWS : (s + 1) * ROWS], 0.0)
        rows.append(sum(m[:, q * PAIR : (q + 1) * PAIR] for q in range(1, NZ // 2)) + m[:, :PAIR])
    half = NS // 2
    return jnp.concatenate(
        [rows[s] + pltpu.roll(rows[s + half], RANK, 1) for s in range(half)], axis=0
    )


def spread_rows(total, out_ref):
    mask = row_mask()
    both = (total, pltpu.roll(total, RANK, 1))
    for s in range(NS):
        half, at = s // (NS // 2), s % (NS // 2) * ROWS
        v = both[half][at : at + ROWS]
        out_ref[pl.ds(s * ROWS, ROWS), :] = jnp.where(
            mask, jnp.concatenate([v] * (NZ // 2), axis=1), 0.0
        ).astype(bf16)


def spread_cols(total, out_ref):
    lo = total.T
    hi = jnp.concatenate([lo[RANK:], lo[:RANK]], axis=0)
    both = jnp.concatenate([lo, hi], axis=1)
    col = lax.broadcasted_iota(jnp.int32, (RANK, R), 1)
    for s in range(1, NS):
        col = jnp.where(lax.broadcasted_iota(jnp.int32, (RANK, R), 1) >= s * ROWS, col - ROWS, col)
    for a in range(NZ):
        keep = (col >= a * CAP) & (col < (a + 1) * CAP)
        v = both[(a % 2) * RANK : (a % 2 + 1) * RANK]
        out_ref[pl.ds(a * RANK, RANK), :] = jnp.where(keep, v, 0.0).astype(bf16)


def back_kernel(g, up, out):
    out[...] = fold(dot(g[...], up[...], ((1,), (1,))))


def grad_kernel(a, b, c, d, x, back16, grad, cols):
    @pl.when(pl.program_id(0) == 0)
    def _():
        total = adapter_scale * (a[...] + b[...] + c[...] + d[...])
        spread_rows(total, back16)
        spread_cols(total, cols)

    grad[...] = dot(cols[...], x[...])


def adg_kernel(back16, down, out):
    out[...] = dot(back16[...], down[...]).astype(bf16)


def hid_kernel(x, down, out, acc):
    @pl.when(pl.program_id(0) == 0)
    def _():
        acc[...] = jnp.zeros_like(acc)

    acc[...] += dot(x[...], down[...], ((1,), (1,)))

    @pl.when(pl.program_id(0) == pl.num_programs(0) - 1)
    def _():
        out[...] = fold(acc[...])


def up_kernel(a, b, c, d, g, up, out, grad, rows, cols):
    total = a[...] + b[...] + c[...] + d[...]
    spread_rows(total, rows)
    spread_cols(total, cols)
    out[...] = (adapter_scale * dot(rows[...], up[...])).astype(bf16)
    grad[...] = dot(cols[...], g[...])


def base_grad_kernel(at, own, *refs):
    cots, mine, other, grad = refs[:NT], refs[NT : 2 * NT - 1], refs[2 * NT - 1 : -1], refs[-1]
    step = pl.program_id(0)

    def half(pieces):
        total = dot(cots[0][...], own[...], ((1,), (1,)))
        for cot, w in zip(cots[1:], pieces):
            total = total + dot(cot[...], w[...], ((1,), (1,)))
        grad[...] = total

    @pl.when(step == at[0])
    def _():
        half(mine)

    @pl.when(step != at[0])
    def _():
        half(other)


def base_out_kernel(at, tokens, own, *refs):
    mine, other, parts = refs[: NT - 1], refs[NT - 1 : 2 * NT - 2], refs[2 * NT - 2 :]
    step = pl.program_id(0)

    def half(pieces):
        for p, w in zip(parts, (own,) + pieces):
            v = dot(tokens[...], w[...])

            @pl.when(step == 0)
            def _():
                p[...] = v

            @pl.when(step != 0)
            def _():
                p[...] += v

    @pl.when(step == at[0])
    def _():
        half(mine)

    @pl.when(step != at[0])
    def _():
        half(other)


def final_kernel(route, ret, base, out):
    out[...] = (base[...] + dot(route[...], ret[...], ((0,), (0,)))).astype(bf16)


def cast_kernel(down, up, out):
    feat = down.shape[2]
    out[:, :feat] = down[0].astype(bf16)
    out[:, feat:] = up[0].astype(bf16)


def route_kernel(counts, holder, cot, route, out):
    n = counts.shape[1]
    before = lax.broadcasted_iota(jnp.int32, (n, n), 0) < lax.broadcasted_iota(jnp.int32, (n, n), 1)
    rows = jnp.broadcast_to(counts[...].astype(f32), (16, n)).astype(bf16)
    lower = dot(rows, jnp.where(before, 1.0, 0.0).astype(bf16))[:1].astype(jnp.int32)
    code = lower * 16 + counts[...]
    r = lax.broadcasted_iota(jnp.int32, (ROWS, n), 0)
    zi = sum(jnp.where(r >= q * CAP, 1, 0) for q in range(1, NZ))
    k = (r - zi * CAP)[:, :1]
    tok = lax.broadcasted_iota(jnp.int32, (ROWS, route.shape[1]), 1)
    for s in range(NS):
        mine = jnp.sum(jnp.where(holder[...] == zi * NS + s, code, 0), axis=1, keepdims=True)
        src = jnp.where(k < (mine & 15), lax.shift_right_logical(mine, 4) + k, -1)
        route[pl.ds(s * ROWS, ROWS), :] = jnp.where(tok == src, 1.0, 0.0).astype(bf16)
    out[...] = dot(route[...], cot[...]).astype(bf16)


def run_back(g_rows, all16, feat, keyw):
    return call(
        back_kernel,
        jax.ShapeDtypeStruct((MID, PAIR), f32),
        [whole((R, keyw)), pl.BlockSpec((WIDE, keyw), lambda i: (0, feat // keyw))],
        whole((MID, PAIR)),
        (1,),
    )(g_rows, all16)


def run_grad(parts, x_rows):
    feat = x_rows.shape[1]
    nb = 2
    return call(
        grad_kernel,
        [jax.ShapeDtypeStruct((R, WIDE), bf16), jax.ShapeDtypeStruct((WIDE, feat), f32)],
        [whole((MID, PAIR))] * 4 + [pl.BlockSpec((R, feat // nb), lambda j: (0, j))],
        [whole((R, WIDE)), pl.BlockSpec((WIDE, feat // nb), lambda j: (0, j))],
        (nb,),
        [pltpu.VMEM((WIDE, R), bf16)],
    )(*parts, x_rows)


def run_adg(back16, all16, feat):
    nb = 2
    return call(
        adg_kernel,
        jax.ShapeDtypeStruct((R, feat), bf16),
        [whole((R, WIDE)), pl.BlockSpec((WIDE, feat // nb), lambda j: (0, j))],
        pl.BlockSpec((R, feat // nb), lambda j: (0, j)),
        (nb,),
    )(back16, all16)


def run_hid(x_rows, all16):
    feat = x_rows.shape[1]
    nb = 2
    return call(
        hid_kernel,
        jax.ShapeDtypeStruct((MID, PAIR), f32),
        [
            pl.BlockSpec((R, feat // nb), lambda j: (0, j)),
            pl.BlockSpec((WIDE, feat // nb), lambda j: (0, j)),
        ],
        whole((MID, PAIR)),
        (nb,),
        [pltpu.VMEM((R, WIDE), f32)],
    )(x_rows, all16)


def run_up(parts, g_rows, all16, feat):
    keyw = g_rows.shape[1]
    return call(
        up_kernel,
        [jax.ShapeDtypeStruct((R, keyw), bf16), jax.ShapeDtypeStruct((WIDE, keyw), f32)],
        [whole((MID, PAIR))] * 4
        + [whole((R, keyw)), pl.BlockSpec((WIDE, keyw), lambda i: (0, feat // keyw))],
        [whole((R, keyw)), whole((WIDE, keyw))],
        (1,),
        [pltpu.VMEM((R, WIDE), bf16), pltpu.VMEM((WIDE, R), bf16)],
    )(*parts, g_rows, all16)


def run_base(kernel, at, lead, lead_specs, weight, pieces, outs, out_specs):
    keyw = weight.shape[1]
    half = pieces[0].shape[0]
    own = pl.BlockSpec((half, keyw), lambda i, at: (at[1] * NC + i, 0))
    n = len(pieces)
    first = kernel is base_out_kernel
    return pl.pallas_call(
        kernel,
        out_shape=outs,
        grid_spec=pltpu.PrefetchScalarGridSpec(
            num_scalar_prefetch=1,
            grid=(NC,),
            in_specs=(lead_specs + [own] if first else [own] + lead_specs)
            + [whole((half, keyw))] * n,
            out_specs=out_specs,
        ),
    )(at, *(lead + [weight] if first else [weight] + lead), *pieces)


def run_base_grad(at, weight, cots, pieces):
    rows, keyw = cots[0].shape
    half = pieces[0].shape[0]
    return run_base(
        base_grad_kernel,
        at,
        cots,
        [whole((rows, keyw))] * NT,
        weight,
        pieces,
        jax.ShapeDtypeStruct((rows, NC * half), f32),
        pl.BlockSpec((rows, half), lambda i, at: (0, i)),
    )


def run_base_out(at, weight, tokens, pieces):
    rows = tokens.shape[0]
    half, keyw = pieces[0].shape
    return run_base(
        base_out_kernel,
        at,
        [tokens],
        [pl.BlockSpec((rows, half), lambda i, at: (0, i))],
        weight,
        pieces,
        [jax.ShapeDtypeStruct((rows, keyw), f32)] * NT,
        [whole((rows, keyw))] * NT,
    )


def run_final(route, ret, base):
    rows, feat = base.shape
    half = feat // 2
    return call(
        final_kernel,
        jax.ShapeDtypeStruct((rows, feat), bf16),
        [whole(route.shape)]
        + [pl.BlockSpec((n, half), lambda j: (0, j)) for n in (ret.shape[0], rows)],
        pl.BlockSpec((rows, half), lambda j: (0, j)),
        (2,),
    )(route, ret, base)


def step(
    tokens,
    cotangent,
    frozen_key_weight,
    counts,
    holder_assignment,
    adapter_down_matrix,
    adapter_up_matrix,
    down_first_moment,
    down_second_moment,
    up_first_moment,
    up_second_moment,
):
    tok_rows, feat = tokens.shape
    keyw = cotangent.shape[1]
    rank = adapter_down_matrix.shape[1]
    t = lax.axis_index("t")
    c = lax.axis_index("c")
    z = lax.axis_index("z")

    both16 = call(cast_kernel, jax.ShapeDtypeStruct((rank, feat + keyw), bf16), [VM] * 2)(
        adapter_down_matrix, adapter_up_matrix
    )
    all16 = lax.all_gather(both16, "z", axis=0, tiled=True)

    route, g_send = call(
        route_kernel,
        [jax.ShapeDtypeStruct((R, tok_rows), bf16), jax.ShapeDtypeStruct((R, keyw), bf16)],
        [VM] * 3,
    )(counts, holder_assignment.reshape(1, -1), cotangent)
    x_send = dot(route, tokens, out=bf16)
    x_rows = lax.all_to_all(x_send, ("x", "c"), 0, 0, tiled=True)
    g_rows = lax.all_to_all(g_send, ("x", "c"), 0, 0, tiled=True)

    half = feat // NC
    halves = []
    for k in range(1, NT):
        piece = lax.dynamic_slice(
            frozen_key_weight, (((t + k) % NT) * feat + c * half, 0), (half, keyw)
        )
        halves.append(shift(piece, k))
    other = [lax.ppermute(v, "c", [(0, 1), (1, 0)]) for v in halves]
    cots = [cotangent] + [shift(cotangent, k) for k in range(1, NT)]
    at = jnp.stack([c, t])
    pieces = halves + other
    base_grad = run_base_grad(at, frozen_key_weight, cots, pieces)
    base_out, *outs = run_base_out(at, frozen_key_weight, tokens, pieces)
    for k in range(1, NT):
        base_out = base_out + shift(outs[k - 1], -k)

    def parts_of(own):
        return [own] + [shift(own, k) for k in range(1, NT)]

    back16, grad_part = run_grad(parts_of(run_back(g_rows, all16, feat, keyw)), x_rows)
    grad_down = lax.psum_scatter(grad_part, "z", scatter_dimension=0, tiled=True)
    adapter_grad = run_adg(back16, all16, feat)
    ret_grad = lax.all_to_all(adapter_grad, ("x", "c"), 0, 0, tiled=True)

    hidden = parts_of(run_hid(x_rows, all16))
    adapter_out, up_part = run_up(hidden, g_rows, all16, feat)
    ret_out = lax.all_to_all(adapter_out, ("x", "c"), 0, 0, tiled=True)
    split = up_part.reshape(NZ // 2, 2, rank, keyw)
    keep = lax.dynamic_index_in_dim(split, z % 2, 1, keepdims=False)
    give = lax.dynamic_index_in_dim(split, 1 - z % 2, 1, keepdims=False)
    keep = keep + lax.ppermute(give, "z", [(i, i ^ 1) for i in range(NZ)])
    nq = NZ // 2
    grad_up = lax.dynamic_index_in_dim(keep, z // 2, 0, keepdims=False)
    for k in range(1, nq):
        give = lax.dynamic_index_in_dim(keep, (z // 2 + k) % nq, 0, keepdims=False)
        grad_up = grad_up + lax.ppermute(
            give, "z", [(i, (i // 2 + k) % nq * 2 + i % 2) for i in range(NZ)]
        )

    layer_out = (base_out + dot(route, ret_out, ((0,), (0,)))).astype(bf16)
    input_grad = run_final(route, ret_grad, base_grad)
    fresh_down = optimizer_update(
        adapter_down_matrix[0], down_first_moment[0], down_second_moment[0], grad_down
    )
    fresh_up = optimizer_update(
        adapter_up_matrix[0], up_first_moment[0], up_second_moment[0], adapter_scale * grad_up
    )
    return (layer_out, input_grad) + tuple(v[None] for v in fresh_down + fresh_up)


def solution(mesh):
    split = Mesh(mesh.devices.reshape(NZ, NX, NC, NT), ("z", "x", "c", "t"))
    dp = ("z", "x", "c")
    act = P(dp, "t")
    state = P(dp, None, "t")
    return jax.shard_map(
        step,
        mesh=split,
        in_specs=(act, act, P(None, "t"), P(dp, None), P()) + (state,) * 6,
        out_specs=(act, act) + (state,) * 6,
        check_vma=False,
    )
```

```python
import jax
import jax.numpy as jnp
from jax import lax
from jax.experimental import pallas as pl
from jax.experimental.pallas import tpu as pltpu
from jax.sharding import Mesh, PartitionSpec as P


adapter_scale = 2.0
learn_rate = 0.01
beta_one = 0.9
beta_two = 0.999
adam_eps = 1e-08
adam_step = 10

NZ, NX, NC, NT = 8, 4, 2, 4
NS = NX * NC
CAP = 12
ROWS = NZ * CAP


bf16 = jnp.bfloat16
f32 = jnp.float32
R = NS * ROWS
MID = R // 2
RANK = 64
PAIR = 2 * RANK
WIDE = NZ * RANK


def optimizer_update(weight, moment, second, grad):
    moment_new = beta_one * moment + (1.0 - beta_one) * grad
    second_new = beta_two * second + (1.0 - beta_two) * grad * grad
    first_fix = 1.0 - beta_one**adam_step
    second_fix = 1.0 - beta_two**adam_step
    weight_new = weight - learn_rate * (moment_new / first_fix) / (
        jnp.sqrt(second_new / second_fix) + adam_eps
    )
    return (weight_new, moment_new, second_new)


def shift(v, k):
    return lax.ppermute(v, "t", [(i, (i + k) % NT) for i in range(NT)])


def dot(a, b, dims=((1,), (0,)), out=f32):
    return lax.dot_general(a, b, (dims, ((), ())), preferred_element_type=out)


def call(body, outs, specs=None, out_specs=None, grid=(), scratch=()):
    vm = pl.BlockSpec(memory_space=pltpu.VMEM)
    kw = {}
    if grid:
        kw["grid"] = grid
    one = not isinstance(outs, (tuple, list))
    return pl.pallas_call(
        body,
        out_shape=outs,
        in_specs=specs,
        out_specs=out_specs or (vm if one else [vm] * len(outs)),
        scratch_shapes=list(scratch),
        **kw,
    )


VM = pl.BlockSpec(memory_space=pltpu.VMEM)


def whole(shape):
    return pl.BlockSpec(shape, lambda *_: (0,) * len(shape))


def row_mask():
    r = lax.broadcasted_iota(jnp.int32, (ROWS, WIDE), 0)
    first = lax.shift_right_logical(lax.broadcasted_iota(jnp.int32, (ROWS, WIDE), 1), 6) * CAP
    return (r >= first) & (r < first + CAP)


def fold(v):
    mask = row_mask()
    rows = []
    for s in range(NS):
        m = jnp.where(mask, v[s * ROWS : (s + 1) * ROWS], 0.0)
        rows.append(sum(m[:, q * PAIR : (q + 1) * PAIR] for q in range(1, NZ // 2)) + m[:, :PAIR])
    half = NS // 2
    return jnp.concatenate(
        [rows[s] + pltpu.roll(rows[s + half], RANK, 1) for s in range(half)], axis=0
    )


def spread_rows(total, out_ref):
    mask = row_mask()
    both = (total, pltpu.roll(total, RANK, 1))
    for s in range(NS):
        half, at = s // (NS // 2), s % (NS // 2) * ROWS
        v = both[half][at : at + ROWS]
        out_ref[pl.ds(s * ROWS, ROWS), :] = jnp.where(
            mask, jnp.concatenate([v] * (NZ // 2), axis=1), 0.0
        ).astype(bf16)


def spread_cols(total, out_ref):
    lo = total.T
    hi = jnp.concatenate([lo[RANK:], lo[:RANK]], axis=0)
    both = jnp.concatenate([lo, hi], axis=1)
    col = lax.broadcasted_iota(jnp.int32, (RANK, R), 1)
    for s in range(1, NS):
        col = jnp.where(lax.broadcasted_iota(jnp.int32, (RANK, R), 1) >= s * ROWS, col - ROWS, col)
    for a in range(NZ):
        keep = (col >= a * CAP) & (col < (a + 1) * CAP)
        v = both[(a % 2) * RANK : (a % 2 + 1) * RANK]
        out_ref[pl.ds(a * RANK, RANK), :] = jnp.where(keep, v, 0.0).astype(bf16)


def back_kernel(g, up, out):
    out[...] = fold(dot(g[...], up[...], ((1,), (1,))))


def grad_kernel(a, b, c, d, x, back16, grad, cols):
    @pl.when(pl.program_id(0) == 0)
    def _():
        total = adapter_scale * (a[...] + b[...] + c[...] + d[...])
        spread_rows(total, back16)
        spread_cols(total, cols)

    grad[...] = dot(cols[...], x[...])


def adg_kernel(back16, down, out):
    out[...] = dot(back16[...], down[...]).astype(bf16)


def hid_kernel(x, down, out, acc):
    @pl.when(pl.program_id(0) == 0)
    def _():
        acc[...] = jnp.zeros_like(acc)

    acc[...] += dot(x[...], down[...], ((1,), (1,)))

    @pl.when(pl.program_id(0) == pl.num_programs(0) - 1)
    def _():
        out[...] = fold(acc[...])


def up_kernel(a, b, c, d, g, up, out, grad, rows, cols):
    total = a[...] + b[...] + c[...] + d[...]
    spread_rows(total, rows)
    spread_cols(total, cols)
    out[...] = (adapter_scale * dot(rows[...], up[...])).astype(bf16)
    grad[...] = dot(cols[...], g[...])


def base_grad_kernel(at, own, *refs):
    cots, mine, other, grad = refs[:NT], refs[NT : 2 * NT - 1], refs[2 * NT - 1 : -1], refs[-1]
    step = pl.program_id(0)

    def half(pieces):
        total = dot(cots[0][...], own[...], ((1,), (1,)))
        for cot, w in zip(cots[1:], pieces):
            total = total + dot(cot[...], w[...], ((1,), (1,)))
        grad[...] = total

    @pl.when(step == at[0])
    def _():
        half(mine)

    @pl.when(step != at[0])
    def _():
        half(other)


def base_out_kernel(at, tokens, own, *refs):
    mine, other, parts = refs[: NT - 1], refs[NT - 1 : 2 * NT - 2], refs[2 * NT - 2 :]
    step = pl.program_id(0)

    def half(pieces):
        for p, w in zip(parts, (own,) + pieces):
            v = dot(tokens[...], w[...])

            @pl.when(step == 0)
            def _():
                p[...] = v

            @pl.when(step != 0)
            def _():
                p[...] += v

    @pl.when(step == at[0])
    def _():
        half(mine)

    @pl.when(step != at[0])
    def _():
        half(other)


def final_kernel(route, ret, base, out):
    out[...] = (base[...] + dot(route[...], ret[...], ((0,), (0,)))).astype(bf16)


def cast_kernel(down, up, out):
    feat = down.shape[2]
    out[:, :feat] = down[0].astype(bf16)
    out[:, feat:] = up[0].astype(bf16)


def route_kernel(counts, holder, cot, route, out):
    n = counts.shape[1]
    before = lax.broadcasted_iota(jnp.int32, (n, n), 0) < lax.broadcasted_iota(jnp.int32, (n, n), 1)
    rows = jnp.broadcast_to(counts[...].astype(f32), (16, n)).astype(bf16)
    lower = dot(rows, jnp.where(before, 1.0, 0.0).astype(bf16))[:1].astype(jnp.int32)
    code = lower * 16 + counts[...]
    r = lax.broadcasted_iota(jnp.int32, (ROWS, n), 0)
    zi = sum(jnp.where(r >= q * CAP, 1, 0) for q in range(1, NZ))
    k = (r - zi * CAP)[:, :1]
    tok = lax.broadcasted_iota(jnp.int32, (ROWS, route.shape[1]), 1)
    for s in range(NS):
        mine = jnp.sum(jnp.where(holder[...] == zi * NS + s, code, 0), axis=1, keepdims=True)
        src = jnp.where(k < (mine & 15), lax.shift_right_logical(mine, 4) + k, -1)
        route[pl.ds(s * ROWS, ROWS), :] = jnp.where(tok == src, 1.0, 0.0).astype(bf16)
    out[...] = dot(route[...], cot[...]).astype(bf16)


def run_back(g_rows, all16, feat, keyw):
    return call(
        back_kernel,
        jax.ShapeDtypeStruct((MID, PAIR), f32),
        [whole((R, keyw)), pl.BlockSpec((WIDE, keyw), lambda i: (0, feat // keyw))],
        whole((MID, PAIR)),
        (1,),
    )(g_rows, all16)


def run_grad(parts, x_rows):
    feat = x_rows.shape[1]
    nb = 2
    return call(
        grad_kernel,
        [jax.ShapeDtypeStruct((R, WIDE), bf16), jax.ShapeDtypeStruct((WIDE, feat), f32)],
        [whole((MID, PAIR))] * 4 + [pl.BlockSpec((R, feat // nb), lambda j: (0, j))],
        [whole((R, WIDE)), pl.BlockSpec((WIDE, feat // nb), lambda j: (0, j))],
        (nb,),
        [pltpu.VMEM((WIDE, R), bf16)],
    )(*parts, x_rows)


def run_adg(back16, all16, feat):
    nb = 2
    return call(
        adg_kernel,
        jax.ShapeDtypeStruct((R, feat), bf16),
        [whole((R, WIDE)), pl.BlockSpec((WIDE, feat // nb), lambda j: (0, j))],
        pl.BlockSpec((R, feat // nb), lambda j: (0, j)),
        (nb,),
    )(back16, all16)


def run_hid(x_rows, all16):
    feat = x_rows.shape[1]
    nb = 2
    return call(
        hid_kernel,
        jax.ShapeDtypeStruct((MID, PAIR), f32),
        [
            pl.BlockSpec((R, feat // nb), lambda j: (0, j)),
            pl.BlockSpec((WIDE, feat // nb), lambda j: (0, j)),
        ],
        whole((MID, PAIR)),
        (nb,),
        [pltpu.VMEM((R, WIDE), f32)],
    )(x_rows, all16)


def run_up(parts, g_rows, all16, feat):
    keyw = g_rows.shape[1]
    return call(
        up_kernel,
        [jax.ShapeDtypeStruct((R, keyw), bf16), jax.ShapeDtypeStruct((WIDE, keyw), f32)],
        [whole((MID, PAIR))] * 4
        + [whole((R, keyw)), pl.BlockSpec((WIDE, keyw), lambda i: (0, feat // keyw))],
        [whole((R, keyw)), whole((WIDE, keyw))],
        (1,),
        [pltpu.VMEM((R, WIDE), bf16), pltpu.VMEM((WIDE, R), bf16)],
    )(*parts, g_rows, all16)


def run_base(kernel, at, lead, lead_specs, weight, pieces, outs, out_specs):
    keyw = weight.shape[1]
    half = pieces[0].shape[0]
    own = pl.BlockSpec((half, keyw), lambda i, at: (at[1] * NC + i, 0))
    n = len(pieces)
    first = kernel is base_out_kernel
    return pl.pallas_call(
        kernel,
        out_shape=outs,
        grid_spec=pltpu.PrefetchScalarGridSpec(
            num_scalar_prefetch=1,
            grid=(NC,),
            in_specs=(lead_specs + [own] if first else [own] + lead_specs)
            + [whole((half, keyw))] * n,
            out_specs=out_specs,
        ),
    )(at, *(lead + [weight] if first else [weight] + lead), *pieces)


def run_base_grad(at, weight, cots, pieces):
    rows, keyw = cots[0].shape
    half = pieces[0].shape[0]
    return run_base(
        base_grad_kernel,
        at,
        cots,
        [whole((rows, keyw))] * NT,
        weight,
        pieces,
        jax.ShapeDtypeStruct((rows, NC * half), f32),
        pl.BlockSpec((rows, half), lambda i, at: (0, i)),
    )


def run_base_out(at, weight, tokens, pieces):
    rows = tokens.shape[0]
    half, keyw = pieces[0].shape
    return run_base(
        base_out_kernel,
        at,
        [tokens],
        [pl.BlockSpec((rows, half), lambda i, at: (0, i))],
        weight,
        pieces,
        [jax.ShapeDtypeStruct((rows, keyw), f32)] * NT,
        [whole((rows, keyw))] * NT,
    )


def layer_kernel(route, ret, a, b, c, d, out):
    total = a[...] + b[...] + c[...] + d[...]
    out[...] = (total + dot(route[...], ret[...], ((0,), (0,)))).astype(bf16)


def run_layer(route, ret, parts):
    return call(layer_kernel, jax.ShapeDtypeStruct(parts[0].shape, bf16), [VM] * 6)(
        route, ret, *parts
    )


def run_final(route, ret, base):
    rows, feat = base.shape
    half = feat // 2
    return call(
        final_kernel,
        jax.ShapeDtypeStruct((rows, feat), bf16),
        [whole(route.shape)]
        + [pl.BlockSpec((n, half), lambda j: (0, j)) for n in (ret.shape[0], rows)],
        pl.BlockSpec((rows, half), lambda j: (0, j)),
        (2,),
    )(route, ret, base)


def step(
    tokens,
    cotangent,
    frozen_key_weight,
    counts,
    holder_assignment,
    adapter_down_matrix,
    adapter_up_matrix,
    down_first_moment,
    down_second_moment,
    up_first_moment,
    up_second_moment,
):
    tok_rows, feat = tokens.shape
    keyw = cotangent.shape[1]
    rank = adapter_down_matrix.shape[1]
    t = lax.axis_index("t")
    c = lax.axis_index("c")
    z = lax.axis_index("z")

    both16 = call(cast_kernel, jax.ShapeDtypeStruct((rank, feat + keyw), bf16), [VM] * 2)(
        adapter_down_matrix, adapter_up_matrix
    )
    all16 = lax.all_gather(both16, "z", axis=0, tiled=True)

    route, g_send = call(
        route_kernel,
        [jax.ShapeDtypeStruct((R, tok_rows), bf16), jax.ShapeDtypeStruct((R, keyw), bf16)],
        [VM] * 3,
    )(counts, holder_assignment.reshape(1, -1), cotangent)
    x_send = dot(route, tokens, out=bf16)
    x_rows = lax.all_to_all(x_send, ("x", "c"), 0, 0, tiled=True)
    g_rows = lax.all_to_all(g_send, ("x", "c"), 0, 0, tiled=True)

    half = feat // NC
    halves = []
    for k in range(1, NT):
        piece = lax.dynamic_slice(
            frozen_key_weight, (((t + k) % NT) * feat + c * half, 0), (half, keyw)
        )
        halves.append(shift(piece, k))
    other = [lax.ppermute(v, "c", [(0, 1), (1, 0)]) for v in halves]
    cots = [cotangent] + [shift(cotangent, k) for k in range(1, NT)]
    at = jnp.stack([c, t])
    pieces = halves + other
    base_grad = run_base_grad(at, frozen_key_weight, cots, pieces)
    base_out, *outs = run_base_out(at, frozen_key_weight, tokens, pieces)
    base_parts = [base_out] + [shift(outs[k - 1], -k) for k in range(1, NT)]

    def parts_of(own):
        return [own] + [shift(own, k) for k in range(1, NT)]

    back16, grad_part = run_grad(parts_of(run_back(g_rows, all16, feat, keyw)), x_rows)
    grad_down = lax.psum_scatter(grad_part, "z", scatter_dimension=0, tiled=True)
    adapter_grad = run_adg(back16, all16, feat)
    ret_grad = lax.all_to_all(adapter_grad, ("x", "c"), 0, 0, tiled=True)

    hidden = parts_of(run_hid(x_rows, all16))
    adapter_out, up_part = run_up(hidden, g_rows, all16, feat)
    ret_out = lax.all_to_all(adapter_out, ("x", "c"), 0, 0, tiled=True)
    split = up_part.reshape(NZ // 2, 2, rank, keyw)
    keep = lax.dynamic_index_in_dim(split, z % 2, 1, keepdims=False)
    give = lax.dynamic_index_in_dim(split, 1 - z % 2, 1, keepdims=False)
    keep = keep + lax.ppermute(give, "z", [(i, i ^ 1) for i in range(NZ)])
    nq = NZ // 2
    grad_up = lax.dynamic_index_in_dim(keep, z // 2, 0, keepdims=False)
    for k in range(1, nq):
        give = lax.dynamic_index_in_dim(keep, (z // 2 + k) % nq, 0, keepdims=False)
        grad_up = grad_up + lax.ppermute(
            give, "z", [(i, (i // 2 + k) % nq * 2 + i % 2) for i in range(NZ)]
        )

    layer_out = run_layer(route, ret_out, base_parts)
    input_grad = run_final(route, ret_grad, base_grad)
    fresh_down = optimizer_update(
        adapter_down_matrix[0], down_first_moment[0], down_second_moment[0], grad_down
    )
    fresh_up = optimizer_update(
        adapter_up_matrix[0], up_first_moment[0], up_second_moment[0], adapter_scale * grad_up
    )
    return (layer_out, input_grad) + tuple(v[None] for v in fresh_down + fresh_up)


def solution(mesh):
    split = Mesh(mesh.devices.reshape(NZ, NX, NC, NT), ("z", "x", "c", "t"))
    dp = ("z", "x", "c")
    act = P(dp, "t")
    state = P(dp, None, "t")
    return jax.shard_map(
        step,
        mesh=split,
        in_specs=(act, act, P(None, "t"), P(dp, None), P()) + (state,) * 6,
        out_specs=(act, act) + (state,) * 6,
        check_vma=False,
    )
```

```python
import jax
import jax.numpy as jnp
from jax import lax
from jax.experimental import pallas as pl
from jax.experimental.pallas import tpu as pltpu
from jax.sharding import Mesh, PartitionSpec as P


adapter_scale = 2.0
learn_rate = 0.01
beta_one = 0.9
beta_two = 0.999
adam_eps = 1e-08
adam_step = 10

NZ, NX, NC, NT = 8, 4, 2, 4
NS = NX * NC
CAP = 12
ROWS = NZ * CAP


bf16 = jnp.bfloat16
f32 = jnp.float32
R = NS * ROWS
MID = R // 2
RANK = 64
PAIR = 2 * RANK
WIDE = NZ * RANK


def optimizer_update(weight, moment, second, grad):
    moment_new = beta_one * moment + (1.0 - beta_one) * grad
    second_new = beta_two * second + (1.0 - beta_two) * grad * grad
    first_fix = 1.0 - beta_one**adam_step
    second_fix = 1.0 - beta_two**adam_step
    weight_new = weight - learn_rate * (moment_new / first_fix) / (
        jnp.sqrt(second_new / second_fix) + adam_eps
    )
    return (weight_new, moment_new, second_new)


def shift(v, k):
    return lax.ppermute(v, "t", [(i, (i + k) % NT) for i in range(NT)])


def dot(a, b, dims=((1,), (0,)), out=f32):
    return lax.dot_general(a, b, (dims, ((), ())), preferred_element_type=out)


def call(body, outs, specs=None, out_specs=None, grid=(), scratch=()):
    vm = pl.BlockSpec(memory_space=pltpu.VMEM)
    kw = {}
    if grid:
        kw["grid"] = grid
    one = not isinstance(outs, (tuple, list))
    return pl.pallas_call(
        body,
        out_shape=outs,
        in_specs=specs,
        out_specs=out_specs or (vm if one else [vm] * len(outs)),
        scratch_shapes=list(scratch),
        **kw,
    )


VM = pl.BlockSpec(memory_space=pltpu.VMEM)


def whole(shape):
    return pl.BlockSpec(shape, lambda *_: (0,) * len(shape))


def row_mask():
    r = lax.broadcasted_iota(jnp.int32, (ROWS, WIDE), 0)
    first = lax.shift_right_logical(lax.broadcasted_iota(jnp.int32, (ROWS, WIDE), 1), 6) * CAP
    return (r >= first) & (r < first + CAP)


def fold(v):
    mask = row_mask()
    rows = []
    for s in range(NS):
        m = jnp.where(mask, v[s * ROWS : (s + 1) * ROWS], 0.0)
        rows.append(sum(m[:, q * PAIR : (q + 1) * PAIR] for q in range(1, NZ // 2)) + m[:, :PAIR])
    half = NS // 2
    return jnp.concatenate(
        [rows[s] + pltpu.roll(rows[s + half], RANK, 1) for s in range(half)], axis=0
    )


def spread_rows(total, out_ref):
    mask = row_mask()
    both = (total, pltpu.roll(total, RANK, 1))
    for s in range(NS):
        half, at = s // (NS // 2), s % (NS // 2) * ROWS
        v = both[half][at : at + ROWS]
        out_ref[pl.ds(s * ROWS, ROWS), :] = jnp.where(
            mask, jnp.concatenate([v] * (NZ // 2), axis=1), 0.0
        ).astype(bf16)


def spread_cols(total, out_ref):
    lo = total.T
    hi = jnp.concatenate([lo[RANK:], lo[:RANK]], axis=0)
    both = jnp.concatenate([lo, hi], axis=1)
    col = lax.broadcasted_iota(jnp.int32, (RANK, R), 1)
    for s in range(1, NS):
        col = jnp.where(lax.broadcasted_iota(jnp.int32, (RANK, R), 1) >= s * ROWS, col - ROWS, col)
    for a in range(NZ):
        keep = (col >= a * CAP) & (col < (a + 1) * CAP)
        v = both[(a % 2) * RANK : (a % 2 + 1) * RANK]
        out_ref[pl.ds(a * RANK, RANK), :] = jnp.where(keep, v, 0.0).astype(bf16)


def back_kernel(g, up, out):
    out[...] = fold(dot(g[...], up[...], ((1,), (1,))))


def grad_kernel(a, b, c, d, x, back16, grad, cols):
    @pl.when(pl.program_id(0) == 0)
    def _():
        total = adapter_scale * (a[...] + b[...] + c[...] + d[...])
        spread_rows(total, back16)
        spread_cols(total, cols)

    grad[...] = dot(cols[...], x[...])


def adg_kernel(back16, down, out):
    out[...] = dot(back16[...], down[...]).astype(bf16)


def hid_kernel(x, down, out, acc):
    @pl.when(pl.program_id(0) == 0)
    def _():
        acc[...] = jnp.zeros_like(acc)

    acc[...] += dot(x[...], down[...], ((1,), (1,)))

    @pl.when(pl.program_id(0) == pl.num_programs(0) - 1)
    def _():
        out[...] = fold(acc[...])


def up_kernel(a, b, c, d, g, up, out, grad, rows, cols):
    total = a[...] + b[...] + c[...] + d[...]
    spread_rows(total, rows)
    spread_cols(total, cols)
    out[...] = (adapter_scale * dot(rows[...], up[...])).astype(bf16)
    grad[...] = dot(cols[...], g[...])


def base_grad_kernel(at, own, *refs):
    cots, mine, other, grad = refs[:NT], refs[NT : 2 * NT - 1], refs[2 * NT - 1 : -1], refs[-1]
    step = pl.program_id(0)

    def half(pieces):
        total = dot(cots[0][...], own[...], ((1,), (1,)))
        for cot, w in zip(cots[1:], pieces):
            total = total + dot(cot[...], w[...], ((1,), (1,)))
        grad[...] = total

    @pl.when(step == at[0])
    def _():
        half(mine)

    @pl.when(step != at[0])
    def _():
        half(other)


def base_out_kernel(at, tokens, own, *refs):
    mine, other, parts = refs[: NT - 1], refs[NT - 1 : 2 * NT - 2], refs[2 * NT - 2 :]
    step = pl.program_id(0)

    def half(pieces):
        keyw = own.shape[1]
        w = jnp.concatenate([v[...] for v in (own,) + pieces], axis=1)
        total = dot(tokens[...], w)
        for k, p in enumerate(parts):
            v = total[:, k * keyw : (k + 1) * keyw]

            @pl.when(step == 0)
            def _():
                p[...] = v

            @pl.when(step != 0)
            def _():
                p[...] += v

    @pl.when(step == at[0])
    def _():
        half(mine)

    @pl.when(step != at[0])
    def _():
        half(other)


def final_kernel(route, ret, base, out):
    out[...] = (base[...] + dot(route[...], ret[...], ((0,), (0,)))).astype(bf16)


def cast_kernel(down, up, out):
    feat = down.shape[2]
    out[:, :feat] = down[0].astype(bf16)
    out[:, feat:] = up[0].astype(bf16)


def route_kernel(counts, holder, cot, route, out):
    n = counts.shape[1]
    before = lax.broadcasted_iota(jnp.int32, (n, n), 0) < lax.broadcasted_iota(jnp.int32, (n, n), 1)
    rows = jnp.broadcast_to(counts[...].astype(f32), (16, n)).astype(bf16)
    lower = dot(rows, jnp.where(before, 1.0, 0.0).astype(bf16))[:1].astype(jnp.int32)
    code = lower * 16 + counts[...]
    r = lax.broadcasted_iota(jnp.int32, (ROWS, n), 0)
    zi = sum(jnp.where(r >= q * CAP, 1, 0) for q in range(1, NZ))
    k = (r - zi * CAP)[:, :1]
    tok = lax.broadcasted_iota(jnp.int32, (ROWS, route.shape[1]), 1)
    for s in range(NS):
        mine = jnp.sum(jnp.where(holder[...] == zi * NS + s, code, 0), axis=1, keepdims=True)
        src = jnp.where(k < (mine & 15), lax.shift_right_logical(mine, 4) + k, -1)
        route[pl.ds(s * ROWS, ROWS), :] = jnp.where(tok == src, 1.0, 0.0).astype(bf16)
    out[...] = dot(route[...], cot[...]).astype(bf16)


def run_back(g_rows, all16, feat, keyw):
    return call(
        back_kernel,
        jax.ShapeDtypeStruct((MID, PAIR), f32),
        [whole((R, keyw)), pl.BlockSpec((WIDE, keyw), lambda i: (0, feat // keyw))],
        whole((MID, PAIR)),
        (1,),
    )(g_rows, all16)


def run_grad(parts, x_rows):
    feat = x_rows.shape[1]
    nb = 2
    return call(
        grad_kernel,
        [jax.ShapeDtypeStruct((R, WIDE), bf16), jax.ShapeDtypeStruct((WIDE, feat), f32)],
        [whole((MID, PAIR))] * 4 + [pl.BlockSpec((R, feat // nb), lambda j: (0, j))],
        [whole((R, WIDE)), pl.BlockSpec((WIDE, feat // nb), lambda j: (0, j))],
        (nb,),
        [pltpu.VMEM((WIDE, R), bf16)],
    )(*parts, x_rows)


def run_adg(back16, all16, feat):
    nb = 2
    return call(
        adg_kernel,
        jax.ShapeDtypeStruct((R, feat), bf16),
        [whole((R, WIDE)), pl.BlockSpec((WIDE, feat // nb), lambda j: (0, j))],
        pl.BlockSpec((R, feat // nb), lambda j: (0, j)),
        (nb,),
    )(back16, all16)


def run_hid(x_rows, all16):
    feat = x_rows.shape[1]
    nb = 2
    return call(
        hid_kernel,
        jax.ShapeDtypeStruct((MID, PAIR), f32),
        [
            pl.BlockSpec((R, feat // nb), lambda j: (0, j)),
            pl.BlockSpec((WIDE, feat // nb), lambda j: (0, j)),
        ],
        whole((MID, PAIR)),
        (nb,),
        [pltpu.VMEM((R, WIDE), f32)],
    )(x_rows, all16)


def run_up(parts, g_rows, all16, feat):
    keyw = g_rows.shape[1]
    return call(
        up_kernel,
        [jax.ShapeDtypeStruct((R, keyw), bf16), jax.ShapeDtypeStruct((WIDE, keyw), f32)],
        [whole((MID, PAIR))] * 4
        + [whole((R, keyw)), pl.BlockSpec((WIDE, keyw), lambda i: (0, feat // keyw))],
        [whole((R, keyw)), whole((WIDE, keyw))],
        (1,),
        [pltpu.VMEM((R, WIDE), bf16), pltpu.VMEM((WIDE, R), bf16)],
    )(*parts, g_rows, all16)


def run_base(kernel, at, lead, lead_specs, weight, pieces, outs, out_specs):
    keyw = weight.shape[1]
    half = pieces[0].shape[0]
    own = pl.BlockSpec((half, keyw), lambda i, at: (at[1] * NC + i, 0))
    n = len(pieces)
    first = kernel is base_out_kernel
    return pl.pallas_call(
        kernel,
        out_shape=outs,
        grid_spec=pltpu.PrefetchScalarGridSpec(
            num_scalar_prefetch=1,
            grid=(NC,),
            in_specs=(lead_specs + [own] if first else [own] + lead_specs)
            + [whole((half, keyw))] * n,
            out_specs=out_specs,
        ),
    )(at, *(lead + [weight] if first else [weight] + lead), *pieces)


def run_base_grad(at, weight, cots, pieces):
    rows, keyw = cots[0].shape
    half = pieces[0].shape[0]
    return run_base(
        base_grad_kernel,
        at,
        cots,
        [whole((rows, keyw))] * NT,
        weight,
        pieces,
        jax.ShapeDtypeStruct((rows, NC * half), f32),
        pl.BlockSpec((rows, half), lambda i, at: (0, i)),
    )


def run_base_out(at, weight, tokens, pieces):
    rows = tokens.shape[0]
    half, keyw = pieces[0].shape
    return run_base(
        base_out_kernel,
        at,
        [tokens],
        [pl.BlockSpec((rows, half), lambda i, at: (0, i))],
        weight,
        pieces,
        [jax.ShapeDtypeStruct((rows, keyw), f32)] * NT,
        [whole((rows, keyw))] * NT,
    )


def layer_kernel(route, ret, a, b, c, d, out):
    total = a[...] + b[...] + c[...] + d[...]
    out[...] = (total + dot(route[...], ret[...], ((0,), (0,)))).astype(bf16)


def run_layer(route, ret, parts):
    return call(layer_kernel, jax.ShapeDtypeStruct(parts[0].shape, bf16), [VM] * 6)(
        route, ret, *parts
    )


def run_final(route, ret, base):
    rows, feat = base.shape
    half = feat // 2
    return call(
        final_kernel,
        jax.ShapeDtypeStruct((rows, feat), bf16),
        [whole(route.shape)]
        + [pl.BlockSpec((n, half), lambda j: (0, j)) for n in (ret.shape[0], rows)],
        pl.BlockSpec((rows, half), lambda j: (0, j)),
        (2,),
    )(route, ret, base)


def step(
    tokens,
    cotangent,
    frozen_key_weight,
    counts,
    holder_assignment,
    adapter_down_matrix,
    adapter_up_matrix,
    down_first_moment,
    down_second_moment,
    up_first_moment,
    up_second_moment,
):
    tok_rows, feat = tokens.shape
    keyw = cotangent.shape[1]
    rank = adapter_down_matrix.shape[1]
    t = lax.axis_index("t")
    c = lax.axis_index("c")
    z = lax.axis_index("z")

    both16 = call(cast_kernel, jax.ShapeDtypeStruct((rank, feat + keyw), bf16), [VM] * 2)(
        adapter_down_matrix, adapter_up_matrix
    )
    all16 = lax.all_gather(both16, "z", axis=0, tiled=True)

    route, g_send = call(
        route_kernel,
        [jax.ShapeDtypeStruct((R, tok_rows), bf16), jax.ShapeDtypeStruct((R, keyw), bf16)],
        [VM] * 3,
    )(counts, holder_assignment.reshape(1, -1), cotangent)
    x_send = dot(route, tokens, out=bf16)
    x_rows = lax.all_to_all(x_send, ("x", "c"), 0, 0, tiled=True)
    g_rows = lax.all_to_all(g_send, ("x", "c"), 0, 0, tiled=True)

    half = feat // NC
    halves = []
    for k in range(1, NT):
        piece = lax.dynamic_slice(
            frozen_key_weight, (((t + k) % NT) * feat + c * half, 0), (half, keyw)
        )
        halves.append(shift(piece, k))
    other = [lax.ppermute(v, "c", [(0, 1), (1, 0)]) for v in halves]
    cots = [cotangent] + [shift(cotangent, k) for k in range(1, NT)]
    at = jnp.stack([c, t])
    pieces = halves + other
    base_grad = run_base_grad(at, frozen_key_weight, cots, pieces)
    base_out, *outs = run_base_out(at, frozen_key_weight, tokens, pieces)
    base_parts = [base_out] + [shift(outs[k - 1], -k) for k in range(1, NT)]

    def parts_of(own):
        return [own] + [shift(own, k) for k in range(1, NT)]

    back16, grad_part = run_grad(parts_of(run_back(g_rows, all16, feat, keyw)), x_rows)
    grad_down = lax.psum_scatter(grad_part, "z", scatter_dimension=0, tiled=True)
    adapter_grad = run_adg(back16, all16, feat)
    ret_grad = lax.all_to_all(adapter_grad, ("x", "c"), 0, 0, tiled=True)

    hidden = parts_of(run_hid(x_rows, all16))
    adapter_out, up_part = run_up(hidden, g_rows, all16, feat)
    ret_out = lax.all_to_all(adapter_out, ("x", "c"), 0, 0, tiled=True)
    split = up_part.reshape(NZ // 2, 2, rank, keyw)
    keep = lax.dynamic_index_in_dim(split, z % 2, 1, keepdims=False)
    give = lax.dynamic_index_in_dim(split, 1 - z % 2, 1, keepdims=False)
    keep = keep + lax.ppermute(give, "z", [(i, i ^ 1) for i in range(NZ)])
    nq = NZ // 2
    grad_up = lax.dynamic_index_in_dim(keep, z // 2, 0, keepdims=False)
    for k in range(1, nq):
        give = lax.dynamic_index_in_dim(keep, (z // 2 + k) % nq, 0, keepdims=False)
        grad_up = grad_up + lax.ppermute(
            give, "z", [(i, (i // 2 + k) % nq * 2 + i % 2) for i in range(NZ)]
        )

    layer_out = run_layer(route, ret_out, base_parts)
    input_grad = run_final(route, ret_grad, base_grad)
    fresh_down = optimizer_update(
        adapter_down_matrix[0], down_first_moment[0], down_second_moment[0], grad_down
    )
    fresh_up = optimizer_update(
        adapter_up_matrix[0], up_first_moment[0], up_second_moment[0], adapter_scale * grad_up
    )
    return (layer_out, input_grad) + tuple(v[None] for v in fresh_down + fresh_up)


def solution(mesh):
    split = Mesh(mesh.devices.reshape(NZ, NX, NC, NT), ("z", "x", "c", "t"))
    dp = ("z", "x", "c")
    act = P(dp, "t")
    state = P(dp, None, "t")
    return jax.shard_map(
        step,
        mesh=split,
        in_specs=(act, act, P(None, "t"), P(dp, None), P()) + (state,) * 6,
        out_specs=(act, act) + (state,) * 6,
        check_vma=False,
    )
```
